32 devices in a mesh: grp: 2 (over x), seq: 16 (over z, y, core).
Axes of the slice: x: 2, y: 2, z: 4, core: 2. Of those that a mesh axis runs over, the one named last changes fastest.
Arguments:
- inputs: bfloat16 [4096, 4096], P(('grp', 'seq')), parts along dimension 0, may hold values from -6 to 6
- in_weight: bfloat16 [4096, 768], replicated, may hold values from -0.09375 to 0.09375
- filter_taps: float32 [2048, 256], P('seq'), may hold values from -6 to 6
- grad_out: bfloat16 [4096, 256], P(('grp', 'seq')), parts along dimension 0, may hold values from -6 to 6
Outputs:
- grad_inputs: bfloat16 [4096, 4096], P(('grp', 'seq')), parts along dimension 0
- grad_weight: float32 [8192, 768], P(('grp', 'seq')), parts along dimension 0
- grad_taps: float32 [4096, 256], P(('grp', 'seq')), parts along dimension 0
The draws below stay inside these ranges and needn't reach their ends.
There are 2 independent parts, one for each index of `grp`. The reference program is written for one: setup_inputs(seed, part) draws one part's arguments, and reference() takes and returns one part's arrays. A program takes and returns all parts, laid end to end along the dimension named above; an argument that names none is the same for every part. Nothing has to cross between parts.
All inputs are finite; a program needn't handle non-finite values.
Results may differ from the reference program's by a relative error of at most 0.0064.
Values sent between devices are 32-bit elements; how exact they have to be, the bound alone decides.
A program may use at most 128 MiB of HBM per device.

```python
import math
import jax
import jax.numpy as jnp
from jax import lax

D = 4096
CH = 256
SEQ = 2048


def raised(result, stream_key, source, target, parts, factor):
    def block_of(axis_at):
        return (jnp.arange(result.shape[axis_at]) // (result.shape[axis_at] // parts)).reshape((-1,) + (1,) * (result.ndim - 1 - axis_at))

    first = jax.random.permutation(stream_key, parts)[block_of(target)]
    second = (block_of(target) + parts // 2) % parts
    return jnp.where((block_of(source) == first) | (block_of(source) == second), factor * result, result)


def shard_levels(stream_key, dims, cuts, smallest, high):
    gain = 1.0
    for position, parts in cuts:
        steps = jax.random.uniform(jax.random.fold_in(jax.random.fold_in(stream_key, 6), position), (parts,), jnp.float32, smallest / len(cuts), high / len(cuts))
        gain = gain * jnp.repeat(jnp.exp(steps), dims[position] // parts).reshape((-1,) + (1,) * (len(dims) - 1 - position))
    return gain


def normal_values(own_key, shape, width, limit, split=(), kind=jnp.bfloat16):
    level = shard_levels(own_key, shape, split, -0.22, 0.18) if split else 1.0
    drawn = jax.random.normal(own_key, shape, jnp.float32) * width * level
    return jnp.minimum(jnp.maximum(drawn, -limit), limit).astype(kind)


def heavy_noise(own_key, shape, spread, bound, split, heavy, kind=jnp.bfloat16):
    drawn = spread * jax.random.normal(own_key, shape, jnp.float32)
    if split:
        drawn = drawn * shard_levels(own_key, shape, split, -0.22, 0.18)
    return jnp.clip(raised(drawn, jax.random.fold_in(own_key, 3), *heavy), -bound, bound).astype(kind)


def setup_inputs(seed: int = 0, part: int = 0) -> dict:
    seeds = jax.random.split(jax.random.key(seed), 5)
    part_keys = jax.random.split(jax.random.fold_in(seeds[4], part), 5)
    inputs = heavy_noise(part_keys[0], (SEQ, D), 1.0, 6.0, ((0, 16),), (0, 1, 16, 2.0))
    in_weight = normal_values(seeds[1], (D, 3 * CH), D ** -0.5, 0.09375)
    filter_taps = normal_values(seeds[2], (SEQ, CH), 1.0, 6.0, ((0, 16),), jnp.float32)
    grad_out = normal_values(part_keys[3], (SEQ, CH), 1.0, 6.0, ((0, 16),))
    return {"inputs": inputs, "in_weight": in_weight, "filter_taps": filter_taps, "grad_out": grad_out}


def reference(inputs, in_weight, filter_taps, grad_out):
    seqlen = inputs.shape[0]
    channels = filter_taps.shape[1]
    scaling = 1.0 / math.sqrt(seqlen)
    projected = jnp.dot(inputs, in_weight, preferred_element_type=jnp.float32).astype(jnp.bfloat16)
    query_rows = projected[:, :channels].astype(jnp.float32)
    key_rows = projected[:, channels:2 * channels].astype(jnp.float32)
    value_rows = projected[:, 2 * channels:].astype(jnp.float32)
    gated_input = key_rows * value_rows
    kernel = filter_taps * scaling
    back_grad = grad_out.astype(jnp.float32) * query_rows
    fft_length = 2 * seqlen
    kernel_spec = jnp.fft.rfft(kernel, n=fft_length, axis=0)
    gated_spec = jnp.fft.rfft(gated_input, n=fft_length, axis=0)
    back_spec = jnp.fft.rfft(back_grad, n=fft_length, axis=0)
    mixed_rows = jnp.fft.irfft(kernel_spec * gated_spec, n=fft_length, axis=0)[:seqlen]
    back_conv = jnp.fft.irfft(jnp.conj(kernel_spec) * back_spec, n=fft_length, axis=0)[:seqlen]
    grad_taps = jnp.fft.irfft(back_spec * jnp.conj(gated_spec), n=fft_length, axis=0)[:seqlen] * scaling
    grad_proj = jnp.concatenate([grad_out.astype(jnp.float32) * mixed_rows, back_conv * value_rows, back_conv * key_rows], axis=1).astype(jnp.bfloat16)
    grad_inputs = lax.dot_general(grad_proj, in_weight, (((1,), (1,)), ((), ())), preferred_element_type=jnp.float32).astype(jnp.bfloat16)
    grad_weight = lax.dot_general(inputs, grad_proj, (((0,), (0,)), ((), ())), preferred_element_type=jnp.float32) * scaling
    return (grad_inputs, grad_weight, grad_taps.astype(jnp.float32))
```

```python
import functools
import math

import jax
import jax.numpy as jnp
from jax import lax
from jax.experimental import pallas as pl
from jax.experimental.pallas import tpu as pltpu
from jax.sharding import PartitionSpec as P

GROUP = 16
TEAM = 8
CHIPS = 4
HALVES = 2
KINDS = 3
PARTS = HALVES * KINDS
PIECES = 4


def round_up(value, step):
    return (value + step - 1) // step * step


def remote(src, dst, send_sem, recv_sem, peer):
    return pltpu.make_async_remote_copy(
        src_ref=src,
        dst_ref=dst,
        send_sem=send_sem,
        recv_sem=recv_sem,
        device_id={"seq": peer},
        device_id_type=pl.DeviceIdType.MESH,
    )


def fused_kernel(
    n, scaling, x_hbm, weight_hbm, taps_hbm, grad_hbm,
    grad_inputs_ref, out_ref, grad_taps_ref,
    x_ref, weights, taps_ref, grad_ref,
    send_taps, send_gated, send_back, got_taps, got_gated, got_back,
    made_mixed, made_conv, made_taps, home_mixed, home_conv, home_taps,
    pad_gated, pad_back, send_cols, got_cols, left, key_rows, value_rows,
    proj_all, made, got,
    load_sems, weight_sems, taps_sems, go_sems, come_sems, back_sems, home_sems,
    send_cols_sems, recv_cols_sems, send_sems, recv_sems, send_sum_sems, recv_sum_sems,
):
    f32, bf16 = jnp.float32, jnp.bfloat16
    me = lax.axis_index("seq")
    rows, depth = x_ref.shape
    channels = taps_ref.shape[1]
    width = channels // HALVES
    cph = width // n
    slim = round_up(cph, 8)
    teams = n // TEAM
    team, mine = me // TEAM, lax.rem(me, TEAM)
    base, chip, core = team * TEAM, mine // 2, lax.rem(mine, 2)
    sibling = chip * 2 + 1 - core
    block = depth // n
    piece = depth // PIECES

    def slot(ref, index, height):
        return ref.at[pl.ds(pl.multiple_of(index * height, 8), height), :]

    def cell(ref, index, half):
        return slot(ref, index * HALVES + half, slim)

    def load(k):
        span = pl.ds(k * piece, piece)
        return pltpu.make_async_copy(
            weight_hbm.at[span, :], weights.at[span, :], weight_sems.at[k]
        )

    barrier = pltpu.get_barrier_semaphore()

    @pl.loop(1, n)
    def _(o):
        pl.semaphore_signal(
            barrier, inc=1, device_id={"seq": lax.rem(me + o, n)},
            device_id_type=pl.DeviceIdType.MESH,
        )

    load_taps = pltpu.make_async_copy(taps_hbm, taps_ref, load_sems.at[0])
    load_x = pltpu.make_async_copy(x_hbm, x_ref, load_sems.at[1])
    load_grad = pltpu.make_async_copy(grad_hbm, grad_ref, load_sems.at[2])
    load_taps.start()
    load_x.start()
    load_grad.start()
    for k in range(PIECES):
        load(k).start()

    def spread(ref, values):
        for p in range(n):
            for h in range(HALVES):
                at, first = (p * HALVES + h) * slim, h * width + p * cph
                ref[at : at + cph, :] = values[first : first + cph, :]

    def gather(ref, h):
        return jnp.concatenate(
            [
                ref[(p * HALVES + h) * slim : (p * HALVES + h) * slim + cph, :]
                for p in range(n)
            ],
            axis=0,
        )

    anti = (
        lax.broadcasted_iota(jnp.int32, (rows, rows), 0)
        + lax.broadcasted_iota(jnp.int32, (rows, rows), 1)
        == rows - 1
    ).astype(f32)

    def reverse(values):
        return jnp.dot(
            values, anti, preferred_element_type=f32, precision=lax.Precision.HIGHEST
        )

    def taps_copy(peer, sender):
        return (remote(slot(send_taps, peer, HALVES * slim), slot(got_taps, sender, HALVES * slim),
                       taps_sems.at[0, peer], taps_sems.at[1, sender], peer),)

    def forth(h):
        def plan(peer, sender):
            return (
                remote(cell(send_gated, peer, h), cell(got_gated, sender, h),
                       go_sems.at[2 * h, peer], come_sems.at[2 * h, sender], peer),
                remote(cell(send_back, peer, h), cell(got_back, n - 1 - sender, h),
                       go_sems.at[2 * h + 1, peer], come_sems.at[2 * h + 1, sender], peer),
            )
        return plan

    def home(h):
        def plan(peer, sender):
            return (
                remote(cell(made_mixed, peer, h), cell(home_mixed, sender, h),
                       back_sems.at[3 * h, peer], home_sems.at[3 * h, sender], peer),
                remote(cell(made_conv, n - 1 - peer, h), cell(home_conv, sender, h),
                       back_sems.at[3 * h + 1, peer], home_sems.at[3 * h + 1, sender], peer),
            )
        return plan

    def home_last(h):
        def plan(peer, sender):
            return (remote(cell(made_taps, n - 1 - peer, h), cell(home_taps, sender, h),
                           back_sems.at[3 * h + 2, peer], home_sems.at[3 * h + 2, sender], peer),)
        return plan

    def exchange_start(plan):
        @pl.loop(1, n)
        def _(k):
            o = n - k
            peer = lax.rem(team + o // TEAM, teams) * TEAM + lax.rem(mine + o, TEAM)
            for copy in plan(peer, me):
                copy.start()

    def exchange_wait(plan):
        @pl.loop(1, n)
        def _(o):
            other = lax.rem(me + n - o, n)
            for copy in plan(other, other):
                copy.wait_recv()

    def exchange_sent(plan):
        @pl.loop(1, n)
        def _(o):
            for copy in plan(lax.rem(me + o, n), me):
                copy.wait_send()

    def cols(peer, index, sender):
        return remote(slot(send_cols, peer * teams + index, rows),
                      slot(got_cols, sender * teams + index, rows),
                      send_cols_sems.at[peer, index], recv_cols_sems.at[sender, index],
                      base + peer)

    def others_of(first, last, act):
        @pl.loop(first, last)
        def _(t):
            index = lax.rem(team + t, teams)

            @pl.loop(1, TEAM)
            def _(o):
                act(lax.rem(mine + o, TEAM), index)

    def cols_start(first, last):
        others_of(first, last, lambda other, index: cols(other, index, mine).start())

    def cols_wait(first, last):
        others_of(first, last, lambda other, index: cols(other, index, other).wait_recv())

    def cols_sent(first, last):
        others_of(first, last, lambda other, index: cols(other, index, mine).wait_send())

    load_taps.wait()
    spread(send_taps, taps_ref[...].T)
    pl.semaphore_wait(barrier, n - 1)
    exchange_start(taps_copy)
    load_x.wait()
    total = jnp.zeros((rows, KINDS * channels), f32)
    for k in range(PIECES):
        load(k).wait()
        total = total + jnp.dot(
            x_ref[:, k * piece : (k + 1) * piece], weights[k * piece : (k + 1) * piece, :],
            preferred_element_type=f32,
        )
    total = total.astype(bf16).astype(f32)
    load_grad.wait()
    spread(send_gated, (total[:, channels : 2 * channels] * total[:, 2 * channels :]).T)
    spread(send_back, reverse((grad_ref[...].astype(f32) * total[:, :channels]).T))
    for h in range(HALVES):
        exchange_start(forth(h))
    for g in range(TEAM):
        for t in range(teams):
            first = (t * TEAM + g) * block
            at = (g * teams + t) * rows
            send_cols[at : at + rows, :] = x_ref[:, first : first + block].astype(f32)
    cols_start(1, teams)
    key_rows[...] = total[:, channels : 2 * channels]
    value_rows[...] = total[:, 2 * channels :]

    slot(got_cols, mine, teams * rows)[...] = slot(send_cols, mine, teams * rows)[...]
    for source, target, place in (
        (send_taps, got_taps, me),
        (send_gated, got_gated, me),
        (send_back, got_back, n - 1 - me),
    ):
        slot(target, place, HALVES * slim)[...] = slot(source, me, HALVES * slim)[...]
    pad_gated[pl.ds(0, n), :] = jnp.zeros((n, rows), f32)
    pad_back[pl.ds(0, n), :] = jnp.zeros((n, rows), f32)

    lane = lax.broadcasted_iota(jnp.int32, (rows, rows), 1)
    line = lax.broadcasted_iota(jnp.int32, (rows, rows), 0)
    keep = lane >= line
    group = min(GROUP, n)

    def turned(source, at, index):
        row = source[pl.ds(index * HALVES * slim + at, 1), :]
        return pltpu.roll(
            jnp.broadcast_to(row, (rows, rows)), 0, 1, stride=1, stride_axis=0
        )

    def channel(at):
        spot = pl.ds(at, n, stride=HALVES * slim)
        pad_gated[pl.ds(n, n), :] = got_gated[spot, :]
        pad_back[pl.ds(n, n), :] = got_back[spot, :]

        def some_lags(q, total):
            matrices = []
            for source in (got_taps, got_gated):
                if isinstance(q, int):
                    before = jnp.zeros((rows, rows), f32)
                else:
                    before = turned(source, at, jnp.maximum(q * group - 1, 0))
                    before = jnp.where(q == 0, 0.0, before)
                parts = []
                for e in range(group):
                    now = turned(source, at, q * group + e)
                    parts.append(jnp.where(keep, now, before).astype(bf16))
                    before = now
                matrices.append(jnp.concatenate(parts, axis=0))
            table = jnp.concatenate(matrices, axis=1)
            lines = jnp.concatenate(
                [
                    jnp.concatenate(
                        [pad[pl.ds(n - q * group - e, n), :] for e in range(group)], axis=1
                    ).astype(bf16)
                    for pad in (pad_gated, pad_back)
                ],
                axis=0,
            )
            return total + jnp.dot(lines, table, preferred_element_type=f32)

        sums = jnp.zeros((2 * n, 2 * rows), f32)
        if n == group:
            sums = some_lags(0, sums)
        else:
            sums = lax.fori_loop(0, n // group, some_lags, sums)
        made_mixed[spot, :] = sums[:n, :rows]
        made_conv[spot, :] = sums[n:, :rows]
        made_taps[spot, :] = sums[n:, rows:]

    exchange_wait(taps_copy)
    for h in range(HALVES):
        exchange_wait(forth(h))

        @pl.loop(0, cph)
        def _(c):
            channel(h * slim + c)

        exchange_start(home(h))
        exchange_start(home_last(h))

    for source, target, place in (
        (made_mixed, home_mixed, me),
        (made_conv, home_conv, n - 1 - me),
        (made_taps, home_taps, n - 1 - me),
    ):
        slot(target, me, HALVES * slim)[...] = slot(source, place, HALVES * slim)[...]

    def turn_columns(index):
        for s in range(TEAM):
            left[pl.ds(pl.multiple_of(index * block, 16), block), s * rows : (s + 1) * rows] = (
                slot(got_cols, s * teams + index, rows)[...].T.astype(bf16)
            )

    def held(part, member):
        return slot(proj_all, part * TEAM + member, rows)

    def span_of(part):
        first = (part % KINDS) * channels + (part // KINDS) * width
        return slice(first, first + width)

    def make_values(h):
        exchange_wait(home(h))
        conv = reverse(gather(home_conv, h)).T * scaling
        mixed = gather(home_mixed, h).T * scaling
        span = slice(h * width, (h + 1) * width)
        for kind, values in enumerate((
            grad_ref[:, span].astype(f32) * mixed,
            conv * value_rows[:, span],
            conv * key_rows[:, span],
        )):
            held(h * KINDS + kind, mine)[...] = values.astype(bf16).astype(f32)

    side = chip + 1 - 2 * lax.rem(chip, 2)
    pair = lax.rem(chip + 2, CHIPS)
    corner = lax.rem(side + 2, CHIPS)

    def spread_copy(part, k):
        member, target = (
            (mine, pair * 2 + core),
            (mine, side * 2 + core),
            (mine, sibling),
            (pair * 2 + core, side * 2 + core),
            (pair * 2 + core, sibling),
            (side * 2 + core, sibling),
            (corner * 2 + core, sibling),
        )[k]
        return remote(held(part, member), held(part, member), send_sems.at[part, k],
                      recv_sems.at[part, member], base + target)

    def arrived(part, member):
        remote(held(part, member), held(part, member), send_sems.at[part, 0],
               recv_sems.at[part, member], base + sibling).wait_recv()

    def spread_first(part):
        for k in range(3):
            spread_copy(part, k).start()

    def spread_second(part):
        arrived(part, pair * 2 + core)
        spread_copy(part, 3).start()
        spread_copy(part, 4).start()
        arrived(part, side * 2 + core)
        spread_copy(part, 5).start()

    def spread_third(part):
        arrived(part, corner * 2 + core)
        spread_copy(part, 6).start()
        arrived(part, sibling)
        for other in (pair, side, corner):
            arrived(part, other * 2 + 1 - core)

    def sums_copy(part, to_team, from_team, peer):
        return remote(slot(made, part * teams + to_team, block),
                      slot(got, part * teams + from_team, block),
                      send_sum_sems.at[part, to_team], recv_sum_sems.at[part, from_team],
                      peer * TEAM + mine)

    def product(part, index):
        lines = left[pl.ds(pl.multiple_of(index * block, 16), block), :]
        right = proj_all[part * TEAM * rows : (part + 1) * TEAM * rows, :].astype(bf16)
        return jnp.dot(lines, right, preferred_element_type=f32)

    def send_products(part):
        @pl.loop(1, teams)
        def _(o):
            target = lax.rem(team + o, teams)
            slot(made, part * teams + target, block)[...] = product(part, target)
            sums_copy(part, target, team, target).start()

    cols_wait(1, teams)

    @pl.loop(1, teams)
    def _(t):
        turn_columns(lax.rem(team + t, teams))

    for h in range(HALVES):
        make_values(h)
        for kind in range(KINDS):
            spread_first(h * KINDS + kind)
        if h == 0:
            cols_start(0, 1)
    for part in range(PARTS + 1):
        if part < PARTS:
            spread_second(part)
        if part > 0:
            spread_third(part - 1)
            send_products(part - 1)

    cols_wait(0, 1)
    turn_columns(team)
    for part in range(PARTS):
        out_ref[:, span_of(part)] = product(part, team)

    tile = min(512, depth)
    lines = jnp.concatenate(
        [
            held(h * KINDS + kind, mine)[...].astype(bf16)
            for kind in range(KINDS)
            for h in range(HALVES)
        ],
        axis=1,
    )

    @pl.loop(0, depth // tile)
    def _(t):
        start = pl.multiple_of(t * tile, tile)
        grad_inputs_ref[:, pl.ds(start, tile)] = lax.dot_general(
            lines, weights[pl.ds(start, tile), :], (((1,), (1,)), ((), ())),
            preferred_element_type=f32,
        ).astype(bf16)

    for h in range(HALVES):
        exchange_wait(home_last(h))
        grad_taps_ref[:, h * width : (h + 1) * width] = reverse(gather(home_taps, h)).T * scaling

    exchange_sent(taps_copy)
    for h in range(HALVES):
        for plan in (forth(h), home(h), home_last(h)):
            exchange_sent(plan)
    cols_sent(0, teams)
    for part in range(PARTS):
        for k in range(7):
            spread_copy(part, k).wait_send()

    for part in range(PARTS):
        span = span_of(part)

        @pl.loop(1, teams)
        def _(o):
            other = lax.rem(team + o, teams)
            sums_copy(part, other, other, other).wait_recv()
            out_ref[:, span] = out_ref[:, span] + slot(got, part * teams + other, block)[...]

        out_ref[:, span] = out_ref[:, span] * scaling

    for part in range(PARTS):
        @pl.loop(1, teams)
        def _(o):
            target = lax.rem(team + o, teams)
            sums_copy(part, target, team, target).wait_send()


def write_kernel(*refs):
    sems = refs[-1]
    copies = [pltpu.make_async_copy(refs[k], refs[3 + k], sems.at[k]) for k in range(3)]
    for copy in copies:
        copy.start()
    for copy in copies:
        copy.wait()


def per_device(inputs, in_weight, filter_taps, grad_out):
    rows, depth = inputs.shape
    channels = filter_taps.shape[1]
    n = lax.axis_size("seq")
    teams = n // TEAM
    scaling = 1.0 / math.sqrt(rows * n)
    width = channels // HALVES
    slim = round_up(width // n, 8)
    block = depth // n
    f32, bf16 = jnp.float32, jnp.bfloat16
    vmem = pl.BlockSpec(memory_space=pltpu.VMEM)
    anywhere = pl.BlockSpec(memory_space=pl.ANY)
    dma = pltpu.SemaphoreType.DMA
    results = pl.pallas_call(
        functools.partial(fused_kernel, n, scaling),
        out_shape=(
            pltpu.VMEM((rows, depth), bf16),
            pltpu.VMEM((block, KINDS * channels), f32),
            pltpu.VMEM((rows, channels), f32),
        ),
        in_specs=[anywhere] * 4,
        out_specs=(vmem,) * 3,
        scratch_shapes=[
            pltpu.VMEM(inputs.shape, inputs.dtype),
            pltpu.VMEM(in_weight.shape, in_weight.dtype),
            pltpu.VMEM(filter_taps.shape, filter_taps.dtype),
            pltpu.VMEM(grad_out.shape, grad_out.dtype),
        ]
        + [pltpu.VMEM((n * HALVES * slim, rows), f32)] * 12
        + [
            pltpu.VMEM((2 * n, rows), f32),
            pltpu.VMEM((2 * n, rows), f32),
            pltpu.VMEM((n * rows, block), f32),
            pltpu.VMEM((n * rows, block), f32),
            pltpu.VMEM((teams * block, TEAM * rows), bf16),
            pltpu.VMEM((rows, channels), f32),
            pltpu.VMEM((rows, channels), f32),
            pltpu.VMEM((PARTS * TEAM * rows, width), f32),
            pltpu.VMEM((PARTS * teams * block, width), f32),
            pltpu.VMEM((PARTS * teams * block, width), f32),
            dma((3,)), dma((PIECES,)), dma((2, n)),
            dma((2 * HALVES, n)), dma((2 * HALVES, n)), dma((3 * HALVES, n)), dma((3 * HALVES, n)),
            dma((TEAM, teams)), dma((TEAM, teams)), dma((PARTS, 7)), dma((PARTS, TEAM)),
            dma((PARTS, teams)), dma((PARTS, teams)),
        ],
        compiler_params=pltpu.CompilerParams(
            collective_id=0, has_side_effects=True, vmem_limit_bytes=117 << 19
        ),
    )(inputs, in_weight, filter_taps, grad_out)
    return pl.pallas_call(
        write_kernel,
        out_shape=tuple(jax.ShapeDtypeStruct(r.shape, r.dtype) for r in results),
        in_specs=[anywhere] * 3,
        out_specs=(anywhere,) * 3,
        scratch_shapes=[dma((3,))],
        compiler_params=pltpu.CompilerParams(vmem_limit_bytes=2 << 20),
    )(*results)


def solution(mesh):
    in_specs = (P(("grp", "seq"), None), P(), P("seq", None), P(("grp", "seq"), None))
    out_specs = (P(("grp", "seq"), None), P(("grp", "seq"), None), P(("grp", "seq"), None))
    return jax.shard_map(
        per_device, mesh=mesh, in_specs=in_specs, out_specs=out_specs, check_vma=False
    )
```

```python
import functools
import math

import jax
import jax.numpy as jnp
from jax import lax
from jax.experimental import pallas as pl
from jax.experimental.pallas import tpu as pltpu
from jax.sharding import PartitionSpec as P

GROUP = 16
TEAM = 8
CHIPS = 4
HALVES = 2
KINDS = 3
PARTS = HALVES * KINDS
PIECES = 4
TAPS, FORTH, HOME, LAST, COLUMNS, SPREAD, SUMS = range(7)


def round_up(value, step):
    return (value + step - 1) // step * step


def remote(src, dst, send_sem, recv_sem, peer):
    return pltpu.make_async_remote_copy(
        src_ref=src,
        dst_ref=dst,
        send_sem=send_sem,
        recv_sem=recv_sem,
        device_id={"seq": peer},
        device_id_type=pl.DeviceIdType.MESH,
    )


def fused_kernel(
    n, scaling, x_hbm, weight_hbm, taps_hbm, grad_hbm,
    grad_inputs_ref, out_ref, grad_taps_ref,
    x_ref, weights, taps_ref, grad_ref,
    send_taps, send_gated, send_back, got_taps, got_gated, got_back,
    made_mixed, made_conv, made_taps, home_mixed, home_conv, home_taps,
    pad_gated, pad_back, send_cols, got_cols, left, key_rows, value_rows,
    proj_all, made, got,
    load_sems, weight_sems, sent_sems, come_sems, recv_cols_sems, recv_sems, recv_sum_sems,
):
    f32, bf16 = jnp.float32, jnp.bfloat16
    me = lax.axis_index("seq")
    rows, depth = x_ref.shape
    channels = taps_ref.shape[1]
    width = channels // HALVES
    cph = width // n
    slim = round_up(cph, 8)
    teams = n // TEAM
    team, mine = me // TEAM, lax.rem(me, TEAM)
    base, chip, core = team * TEAM, mine // 2, lax.rem(mine, 2)
    sibling = chip * 2 + 1 - core
    block = depth // n
    piece = depth // PIECES

    def slot(ref, index, height):
        return ref.at[pl.ds(pl.multiple_of(index * height, 8), height), :]

    def cell(ref, index, half):
        return slot(ref, index * HALVES + half, slim)

    def load(k):
        span = pl.ds(k * piece, piece)
        return pltpu.make_async_copy(
            weight_hbm.at[span, :], weights.at[span, :], weight_sems.at[k]
        )

    barrier = pltpu.get_barrier_semaphore()

    @pl.loop(1, n)
    def _(o):
        pl.semaphore_signal(
            barrier, inc=1, device_id={"seq": lax.rem(me + o, n)},
            device_id_type=pl.DeviceIdType.MESH,
        )

    load_taps = pltpu.make_async_copy(taps_hbm, taps_ref, load_sems.at[0])
    load_x = pltpu.make_async_copy(x_hbm, x_ref, load_sems.at[1])
    load_grad = pltpu.make_async_copy(grad_hbm, grad_ref, load_sems.at[2])
    load_taps.start()
    load_x.start()
    load_grad.start()
    for k in range(PIECES):
        load(k).start()

    def spread(ref, values):
        for p in range(n):
            for h in range(HALVES):
                at, first = (p * HALVES + h) * slim, h * width + p * cph
                ref[at : at + cph, :] = values[first : first + cph, :]

    def gather(ref, h):
        return jnp.concatenate(
            [
                ref[(p * HALVES + h) * slim : (p * HALVES + h) * slim + cph, :]
                for p in range(n)
            ],
            axis=0,
        )

    anti = (
        lax.broadcasted_iota(jnp.int32, (rows, rows), 0)
        + lax.broadcasted_iota(jnp.int32, (rows, rows), 1)
        == rows - 1
    ).astype(f32)

    def reverse(values):
        return jnp.dot(
            values, anti, preferred_element_type=f32, precision=lax.Precision.HIGHEST
        )

    def taps_copy(h):
        def plan(peer, sender):
            return (remote(cell(send_taps, peer, h), cell(got_taps, sender, h),
                           sent_sems.at[TAPS, h], come_sems.at[TAPS, h], peer),)
        return plan

    def forth(h):
        def plan(peer, sender):
            return (
                remote(cell(send_gated, peer, h), cell(got_gated, sender, h),
                       sent_sems.at[FORTH, h], come_sems.at[FORTH, h], peer),
                remote(cell(send_back, peer, h), cell(got_back, n - 1 - sender, h),
                       sent_sems.at[FORTH, h], come_sems.at[FORTH, h], peer),
            )
        return plan

    def home(h):
        def plan(peer, sender):
            return (
                remote(cell(made_mixed, peer, h), cell(home_mixed, sender, h),
                       sent_sems.at[HOME, h], come_sems.at[HOME, h], peer),
                remote(cell(made_conv, n - 1 - peer, h), cell(home_conv, sender, h),
                       sent_sems.at[HOME, h], come_sems.at[HOME, h], peer),
            )
        return plan

    def home_last(h):
        def plan(peer, sender):
            return (remote(cell(made_taps, n - 1 - peer, h), cell(home_taps, sender, h),
                           sent_sems.at[LAST, h], come_sems.at[LAST, h], peer),)
        return plan

    def region(ref, height, send_sem, recv_sem):
        return remote(ref.at[pl.ds(0, height), :], ref.at[pl.ds(0, height), :],
                      send_sem, recv_sem, base + sibling)

    def exchange_start(plan):
        @pl.loop(1, n)
        def _(k):
            o = n - k
            peer = lax.rem(team + o // TEAM, teams) * TEAM + lax.rem(mine + o, TEAM)
            for copy in plan(peer, me):
                copy.start()

    def exchange_wait(kind, h):
        cells = (n - 1) * (2 if kind in (FORTH, HOME) else 1)
        region(got_gated, cells * slim, sent_sems.at[kind, h], come_sems.at[kind, h]).wait_recv()

    def exchange_sent(kind):
        cells = (n - 1) * (2 if kind in (FORTH, HOME) else 1)
        for h in range(HALVES):
            region(got_gated, cells * slim, sent_sems.at[kind, h], come_sems.at[kind, h]).wait_send()

    def cols(peer, index, sender, late):
        return remote(slot(send_cols, peer * teams + index, rows),
                      slot(got_cols, sender * teams + index, rows),
                      sent_sems.at[COLUMNS, 0], recv_cols_sems.at[late], base + peer)

    def cols_start(late):
        @pl.loop(0 if late else 1, 1 if late else teams)
        def _(t):
            @pl.loop(1, TEAM)
            def _(o):
                cols(lax.rem(mine + o, TEAM), lax.rem(team + t, teams), mine, late).start()

    def cols_wait(late):
        blocks = (TEAM - 1) * (1 if late else teams - 1)
        region(got_cols, blocks * rows, sent_sems.at[COLUMNS, 0], recv_cols_sems.at[late]).wait_recv()

    load_taps.wait()
    spread(send_taps, taps_ref[...].T)
    pl.semaphore_wait(barrier, n - 1)
    exchange_start(taps_copy(0))
    load_x.wait()
    total = jnp.zeros((rows, KINDS * channels), f32)
    for k in range(PIECES):
        load(k).wait()
        total = total + jnp.dot(
            x_ref[:, k * piece : (k + 1) * piece], weights[k * piece : (k + 1) * piece, :],
            preferred_element_type=f32,
        )
    total = total.astype(bf16).astype(f32)
    load_grad.wait()
    spread(send_gated, (total[:, channels : 2 * channels] * total[:, 2 * channels :]).T)
    spread(send_back, reverse((grad_ref[...].astype(f32) * total[:, :channels]).T))
    exchange_start(forth(0))
    for h in range(1, HALVES):
        exchange_start(taps_copy(h))
        exchange_start(forth(h))
    for g in range(TEAM):
        for t in range(teams):
            first = (t * TEAM + g) * block
            at = (g * teams + t) * rows
            send_cols[at : at + rows, :] = x_ref[:, first : first + block].astype(f32)
    cols_start(0)
    key_rows[...] = total[:, channels : 2 * channels]
    value_rows[...] = total[:, 2 * channels :]

    slot(got_cols, mine, teams * rows)[...] = slot(send_cols, mine, teams * rows)[...]
    for source, target, place in (
        (send_taps, got_taps, me),
        (send_gated, got_gated, me),
        (send_back, got_back, n - 1 - me),
    ):
        slot(target, place, HALVES * slim)[...] = slot(source, me, HALVES * slim)[...]
    pad_gated[pl.ds(0, n), :] = jnp.zeros((n, rows), f32)
    pad_back[pl.ds(0, n), :] = jnp.zeros((n, rows), f32)

    lane = lax.broadcasted_iota(jnp.int32, (rows, rows), 1)
    line = lax.broadcasted_iota(jnp.int32, (rows, rows), 0)
    keep = lane >= line
    group = min(GROUP, n)

    def turned(source, at, index):
        row = source[pl.ds(index * HALVES * slim + at, 1), :]
        return pltpu.roll(
            jnp.broadcast_to(row, (rows, rows)), 0, 1, stride=1, stride_axis=0
        )

    def channel(at):
        spot = pl.ds(at, n, stride=HALVES * slim)
        pad_gated[pl.ds(n, n), :] = got_gated[spot, :]
        pad_back[pl.ds(n, n), :] = got_back[spot, :]

        def some_lags(q, total):
            matrices = []
            for source in (got_taps, got_gated):
                if isinstance(q, int):
                    before = jnp.zeros((rows, rows), f32)
                else:
                    before = turned(source, at, jnp.maximum(q * group - 1, 0))
                    before = jnp.where(q == 0, 0.0, before)
                parts = []
                for e in range(group):
                    now = turned(source, at, q * group + e)
                    parts.append(jnp.where(keep, now, before).astype(bf16))
                    before = now
                matrices.append(jnp.concatenate(parts, axis=0))
            table = jnp.concatenate(matrices, axis=1)
            lines = jnp.concatenate(
                [
                    jnp.concatenate(
                        [pad[pl.ds(n - q * group - e, n), :] for e in range(group)], axis=1
                    ).astype(bf16)
                    for pad in (pad_gated, pad_back)
                ],
                axis=0,
            )
            return total + jnp.dot(lines, table, preferred_element_type=f32)

        sums = jnp.zeros((2 * n, 2 * rows), f32)
        if n == group:
            sums = some_lags(0, sums)
        else:
            sums = lax.fori_loop(0, n // group, some_lags, sums)
        made_mixed[spot, :] = sums[:n, :rows]
        made_conv[spot, :] = sums[n:, :rows]
        made_taps[spot, :] = sums[n:, rows:]

    for h in range(HALVES):
        exchange_wait(TAPS, h)
        exchange_wait(FORTH, h)

        @pl.loop(0, cph)
        def _(c):
            channel(h * slim + c)

        exchange_start(home(h))
        exchange_start(home_last(h))

    for source, target, place in (
        (made_mixed, home_mixed, me),
        (made_conv, home_conv, n - 1 - me),
        (made_taps, home_taps, n - 1 - me),
    ):
        slot(target, me, HALVES * slim)[...] = slot(source, place, HALVES * slim)[...]

    def turn_columns(index):
        for s in range(TEAM):
            left[pl.ds(pl.multiple_of(index * block, 16), block), s * rows : (s + 1) * rows] = (
                slot(got_cols, s * teams + index, rows)[...].T.astype(bf16)
            )

    def held(part, member):
        return slot(proj_all, part * TEAM + member, rows)

    def span_of(part):
        first = (part % KINDS) * channels + (part // KINDS) * width
        return slice(first, first + width)

    def make_values(h):
        exchange_wait(HOME, h)
        conv = reverse(gather(home_conv, h)).T * scaling
        mixed = gather(home_mixed, h).T * scaling
        span = slice(h * width, (h + 1) * width)
        for kind, values in enumerate((
            grad_ref[:, span].astype(f32) * mixed,
            conv * value_rows[:, span],
            conv * key_rows[:, span],
        )):
            held(h * KINDS + kind, mine)[...] = values.astype(bf16).astype(f32)

    side = chip + 1 - 2 * lax.rem(chip, 2)
    pair = lax.rem(chip + 2, CHIPS)
    corner = lax.rem(side + 2, CHIPS)

    def spread_copy(part, k):
        member, target = (
            (mine, pair * 2 + core),
            (mine, side * 2 + core),
            (mine, sibling),
            (pair * 2 + core, side * 2 + core),
            (pair * 2 + core, sibling),
            (side * 2 + core, sibling),
            (corner * 2 + core, sibling),
        )[k]
        return remote(held(part, member), held(part, member), sent_sems.at[SPREAD, 0],
                      recv_sems.at[part, (0, 1, 3, 2, 3, 3, 3)[k]], base + target)

    def arrived(part, k):
        blocks = TEAM // 2 if k == 3 else 1
        region(proj_all, blocks * rows, sent_sems.at[SPREAD, 0], recv_sems.at[part, k]).wait_recv()

    def spread_first(part):
        for k in range(3):
            spread_copy(part, k).start()

    def spread_second(part):
        arrived(part, 0)
        spread_copy(part, 3).start()
        spread_copy(part, 4).start()
        arrived(part, 1)
        spread_copy(part, 5).start()

    def spread_third(part):
        arrived(part, 2)
        spread_copy(part, 6).start()
        arrived(part, 3)

    def sums_copy(part, to_team, from_team, peer):
        return remote(slot(made, part * teams + to_team, block),
                      slot(got, part * teams + from_team, block),
                      sent_sems.at[SUMS, 0], recv_sum_sems.at[part],
                      peer * TEAM + mine)

    def product(part, index):
        lines = left[pl.ds(pl.multiple_of(index * block, 16), block), :]
        right = proj_all[part * TEAM * rows : (part + 1) * TEAM * rows, :].astype(bf16)
        return jnp.dot(lines, right, preferred_element_type=f32)

    def send_products(part):
        @pl.loop(1, teams)
        def _(o):
            target = lax.rem(team + o, teams)
            slot(made, part * teams + target, block)[...] = product(part, target)
            sums_copy(part, target, team, target).start()

    cols_wait(0)

    @pl.loop(1, teams)
    def _(t):
        turn_columns(lax.rem(team + t, teams))

    for h in range(HALVES):
        make_values(h)
        for kind in range(KINDS):
            spread_first(h * KINDS + kind)
    for part in range(PARTS + 1):
        if part < PARTS:
            spread_second(part)
        if part == KINDS + 1:
            cols_start(1)
        if part > 0:
            spread_third(part - 1)
            send_products(part - 1)

    cols_wait(1)
    turn_columns(team)
    for part in range(PARTS):
        out_ref[:, span_of(part)] = product(part, team)

    tile = min(512, depth)
    lines = jnp.concatenate(
        [
            held(h * KINDS + kind, mine)[...].astype(bf16)
            for kind in range(KINDS)
            for h in range(HALVES)
        ],
        axis=1,
    )

    @pl.loop(0, depth // tile)
    def _(t):
        start = pl.multiple_of(t * tile, tile)
        grad_inputs_ref[:, pl.ds(start, tile)] = lax.dot_general(
            lines, weights[pl.ds(start, tile), :], (((1,), (1,)), ((), ())),
            preferred_element_type=f32,
        ).astype(bf16)

    for h in range(HALVES):
        exchange_wait(LAST, h)
        grad_taps_ref[:, h * width : (h + 1) * width] = reverse(gather(home_taps, h)).T * scaling

    for kind in (TAPS, FORTH, HOME, LAST):
        exchange_sent(kind)
    region(got_cols, (TEAM - 1) * teams * rows, sent_sems.at[COLUMNS, 0],
           recv_cols_sems.at[0]).wait_send()
    region(proj_all, PARTS * 7 * rows, sent_sems.at[SPREAD, 0], recv_sems.at[0, 0]).wait_send()

    for part in range(PARTS):
        span = span_of(part)
        region(got, (teams - 1) * block, sent_sems.at[SUMS, 0], recv_sum_sems.at[part]).wait_recv()

        @pl.loop(1, teams)
        def _(o):
            other = lax.rem(team + o, teams)
            out_ref[:, span] = out_ref[:, span] + slot(got, part * teams + other, block)[...]

        out_ref[:, span] = out_ref[:, span] * scaling

    region(got, PARTS * (teams - 1) * block, sent_sems.at[SUMS, 0], recv_sum_sems.at[0]).wait_send()


def write_kernel(*refs):
    sems = refs[-1]
    copies = [pltpu.make_async_copy(refs[k], refs[3 + k], sems.at[k]) for k in range(3)]
    for copy in copies:
        copy.start()
    for copy in copies:
        copy.wait()


def per_device(inputs, in_weight, filter_taps, grad_out):
    rows, depth = inputs.shape
    channels = filter_taps.shape[1]
    n = lax.axis_size("seq")
    teams = n // TEAM
    scaling = 1.0 / math.sqrt(rows * n)
    width = channels // HALVES
    slim = round_up(width // n, 8)
    block = depth // n
    f32, bf16 = jnp.float32, jnp.bfloat16
    vmem = pl.BlockSpec(memory_space=pltpu.VMEM)
    anywhere = pl.BlockSpec(memory_space=pl.ANY)
    dma = pltpu.SemaphoreType.DMA
    results = pl.pallas_call(
        functools.partial(fused_kernel, n, scaling),
        out_shape=(
            pltpu.VMEM((rows, depth), bf16),
            pltpu.VMEM((block, KINDS * channels), f32),
            pltpu.VMEM((rows, channels), f32),
        ),
        in_specs=[anywhere] * 4,
        out_specs=(vmem,) * 3,
        scratch_shapes=[
            pltpu.VMEM(inputs.shape, inputs.dtype),
            pltpu.VMEM(in_weight.shape, in_weight.dtype),
            pltpu.VMEM(filter_taps.shape, filter_taps.dtype),
            pltpu.VMEM(grad_out.shape, grad_out.dtype),
        ]
        + [pltpu.VMEM((n * HALVES * slim, rows), f32)] * 12
        + [
            pltpu.VMEM((2 * n, rows), f32),
            pltpu.VMEM((2 * n, rows), f32),
            pltpu.VMEM((n * rows, block), f32),
            pltpu.VMEM((n * rows, block), f32),
            pltpu.VMEM((teams * block, TEAM * rows), bf16),
            pltpu.VMEM((rows, channels), f32),
            pltpu.VMEM((rows, channels), f32),
            pltpu.VMEM((PARTS * TEAM * rows, width), f32),
            pltpu.VMEM((PARTS * teams * block, width), f32),
            pltpu.VMEM((PARTS * teams * block, width), f32),
            dma((3,)), dma((PIECES,)), dma((7, HALVES)), dma((4, HALVES)), dma((2,)),
            dma((PARTS, 4)), dma((PARTS,)),
        ],
        compiler_params=pltpu.CompilerParams(
            collective_id=0, has_side_effects=True, vmem_limit_bytes=117 << 19
        ),
    )(inputs, in_weight, filter_taps, grad_out)
    return pl.pallas_call(
        write_kernel,
        out_shape=tuple(jax.ShapeDtypeStruct(r.shape, r.dtype) for r in results),
        in_specs=[anywhere] * 3,
        out_specs=(anywhere,) * 3,
        scratch_shapes=[dma((3,))],
        compiler_params=pltpu.CompilerParams(vmem_limit_bytes=2 << 20),
    )(*results)


def solution(mesh):
    in_specs = (P(("grp", "seq"), None), P(), P("seq", None), P(("grp", "seq"), None))
    out_specs = (P(("grp", "seq"), None), P(("grp", "seq"), None), P(("grp", "seq"), None))
    return jax.shard_map(
        per_device, mesh=mesh, in_specs=in_specs, out_specs=out_specs, check_vma=False
    )
```

```python
import functools
import math

import jax
import jax.numpy as jnp
from jax import lax
from jax.experimental import pallas as pl
from jax.experimental.pallas import tpu as pltpu
from jax.sharding import PartitionSpec as P

GROUP = 16
TEAM = 8
CHIPS = 4
HALVES = 2
KINDS = 3
PARTS = HALVES * KINDS
PIECES = 4
TAPS, FORTH, HOME, LAST, COLUMNS, SPREAD, SUMS = range(7)


def round_up(value, step):
    return (value + step - 1) // step * step


def remote(src, dst, send_sem, recv_sem, peer):
    return pltpu.make_async_remote_copy(
        src_ref=src,
        dst_ref=dst,
        send_sem=send_sem,
        recv_sem=recv_sem,
        device_id={"seq": peer},
        device_id_type=pl.DeviceIdType.MESH,
    )


def fused_kernel(
    n, scaling, x_hbm, weight_hbm, taps_hbm, grad_hbm,
    grad_inputs_ref, out_ref, grad_taps_ref,
    x_ref, weights, taps_ref, grad_ref,
    send_taps, send_gated, send_back, got_taps, got_gated, got_back,
    made_mixed, made_conv, made_taps, home_mixed, home_conv, home_taps,
    pad_gated, pad_back, send_cols, got_cols, left, key_rows, value_rows,
    proj_all, made, got,
    load_sems, weight_sems, sent_sems, come_sems, recv_cols_sems, recv_sems, recv_sum_sems,
):
    f32, bf16 = jnp.float32, jnp.bfloat16
    me = lax.axis_index("seq")
    rows, depth = x_ref.shape
    channels = taps_ref.shape[1]
    width = channels // HALVES
    cph = width // n
    slim = round_up(cph, 8)
    teams = n // TEAM
    team, mine = me // TEAM, lax.rem(me, TEAM)
    base, chip, core = team * TEAM, mine // 2, lax.rem(mine, 2)
    sibling = chip * 2 + 1 - core
    block = depth // n
    piece = depth // PIECES

    def slot(ref, index, height):
        return ref.at[pl.ds(pl.multiple_of(index * height, 8), height), :]

    def cell(ref, index, half):
        return slot(ref, index * HALVES + half, slim)

    def load(k):
        span = pl.ds(k * piece, piece)
        return pltpu.make_async_copy(
            weight_hbm.at[span, :], weights.at[span, :], weight_sems.at[k]
        )

    barrier = pltpu.get_barrier_semaphore()

    @pl.loop(1, n)
    def _(o):
        pl.semaphore_signal(
            barrier, inc=1, device_id={"seq": lax.rem(me + o, n)},
            device_id_type=pl.DeviceIdType.MESH,
        )

    load_taps = pltpu.make_async_copy(taps_hbm, taps_ref, load_sems.at[0])
    load_x = pltpu.make_async_copy(x_hbm, x_ref, load_sems.at[1])
    load_grad = pltpu.make_async_copy(grad_hbm, grad_ref, load_sems.at[2])
    load_taps.start()
    load_x.start()
    load_grad.start()
    for k in range(PIECES):
        load(k).start()

    def spread(ref, values):
        for p in range(n):
            for h in range(HALVES):
                at, first = (p * HALVES + h) * slim, h * width + p * cph
                ref[at : at + cph, :] = values[first : first + cph, :]

    def gather(ref, h):
        return jnp.concatenate(
            [
                ref[(p * HALVES + h) * slim : (p * HALVES + h) * slim + cph, :]
                for p in range(n)
            ],
            axis=0,
        )

    anti = (
        lax.broadcasted_iota(jnp.int32, (rows, rows), 0)
        + lax.broadcasted_iota(jnp.int32, (rows, rows), 1)
        == rows - 1
    ).astype(f32)

    def reverse(values):
        return jnp.dot(
            values, anti, preferred_element_type=f32, precision=lax.Precision.HIGHEST
        )

    def taps_copy(h):
        def plan(peer, sender):
            return (remote(cell(send_taps, peer, h), cell(got_taps, sender, h),
                           sent_sems.at[TAPS, h], come_sems.at[TAPS, h], peer),)
        return plan

    def forth(h):
        def plan(peer, sender):
            return (
                remote(cell(send_gated, peer, h), cell(got_gated, sender, h),
                       sent_sems.at[FORTH, h], come_sems.at[FORTH, h], peer),
                remote(cell(send_back, peer, h), cell(got_back, n - 1 - sender, h),
                       sent_sems.at[FORTH, h], come_sems.at[FORTH, h], peer),
            )
        return plan

    def home(h):
        def plan(peer, sender):
            return (
                remote(cell(made_mixed, peer, h), cell(home_mixed, sender, h),
                       sent_sems.at[HOME, h], come_sems.at[HOME, h], peer),
                remote(cell(made_conv, n - 1 - peer, h), cell(home_conv, sender, h),
                       sent_sems.at[HOME, h], come_sems.at[HOME, h], peer),
            )
        return plan

    def home_last(h):
        def plan(peer, sender):
            return (remote(cell(made_taps, n - 1 - peer, h), cell(home_taps, sender, h),
                           sent_sems.at[LAST, h], come_sems.at[LAST, h], peer),)
        return plan

    def region(ref, height, send_sem, recv_sem):
        return remote(ref.at[pl.ds(0, height), :], ref.at[pl.ds(0, height), :],
                      send_sem, recv_sem, base + sibling)

    def exchange_start(plan):
        @pl.loop(1, n)
        def _(k):
            o = n - k
            peer = lax.rem(team + o // TEAM, teams) * TEAM + lax.rem(mine + o, TEAM)
            for copy in plan(peer, me):
                copy.start()

    def exchange_wait(kind, h):
        cells = (n - 1) * (2 if kind in (FORTH, HOME) else 1)
        region(got_gated, cells * slim, sent_sems.at[kind, h], come_sems.at[kind, h]).wait_recv()

    def exchange_sent(kind):
        cells = (n - 1) * (2 if kind in (FORTH, HOME) else 1)
        for h in range(HALVES):
            region(got_gated, cells * slim, sent_sems.at[kind, h], come_sems.at[kind, h]).wait_send()

    def cols(peer, index, sender, late):
        return remote(slot(send_cols, peer * teams + index, rows),
                      slot(got_cols, sender * teams + index, rows),
                      sent_sems.at[COLUMNS, 0], recv_cols_sems.at[late], base + peer)

    def cols_start(late):
        @pl.loop(0 if late else 1, 1 if late else teams)
        def _(t):
            @pl.loop(1, TEAM)
            def _(o):
                cols(lax.rem(mine + o, TEAM), lax.rem(team + t, teams), mine, late).start()

    def cols_wait(late):
        blocks = (TEAM - 1) * (1 if late else teams - 1)
        region(got_cols, blocks * rows, sent_sems.at[COLUMNS, 0], recv_cols_sems.at[late]).wait_recv()

    load_taps.wait()
    spread(send_taps, taps_ref[...].T)
    pl.semaphore_wait(barrier, n - 1)
    exchange_start(taps_copy(0))
    load_x.wait()
    total = jnp.zeros((rows, KINDS * channels), f32)
    for k in range(PIECES):
        load(k).wait()
        total = total + jnp.dot(
            x_ref[:, k * piece : (k + 1) * piece], weights[k * piece : (k + 1) * piece, :],
            preferred_element_type=f32,
        )
    total = total.astype(bf16).astype(f32)
    load_grad.wait()
    spread(send_gated, (total[:, channels : 2 * channels] * total[:, 2 * channels :]).T)
    spread(send_back, reverse((grad_ref[...].astype(f32) * total[:, :channels]).T))
    exchange_start(forth(0))
    for h in range(1, HALVES):
        exchange_start(taps_copy(h))
        exchange_start(forth(h))
    for g in range(TEAM):
        for t in range(teams):
            first = (t * TEAM + g) * block
            at = (g * teams + t) * rows
            send_cols[at : at + rows, :] = x_ref[:, first : first + block].astype(f32)
    cols_start(0)
    key_rows[...] = total[:, channels : 2 * channels]
    value_rows[...] = total[:, 2 * channels :]

    slot(got_cols, mine, teams * rows)[...] = slot(send_cols, mine, teams * rows)[...]
    for source, target, place in (
        (send_taps, got_taps, me),
        (send_gated, got_gated, me),
        (send_back, got_back, n - 1 - me),
    ):
        slot(target, place, HALVES * slim)[...] = slot(source, me, HALVES * slim)[...]
    pad_gated[pl.ds(0, n), :] = jnp.zeros((n, rows), f32)
    pad_back[pl.ds(0, n), :] = jnp.zeros((n, rows), f32)

    lane = lax.broadcasted_iota(jnp.int32, (rows, rows), 1)
    line = lax.broadcasted_iota(jnp.int32, (rows, rows), 0)
    keep = lane >= line
    group = min(GROUP, n)

    def turned(source, at, index):
        row = source[pl.ds(index * HALVES * slim + at, 1), :]
        return pltpu.roll(
            jnp.broadcast_to(row, (rows, rows)), 0, 1, stride=1, stride_axis=0
        )

    def channel(at):
        spot = pl.ds(at, n, stride=HALVES * slim)
        pad_gated[pl.ds(n, n), :] = got_gated[spot, :]
        pad_back[pl.ds(n, n), :] = got_back[spot, :]

        def some_lags(q, total):
            matrices = []
            for source in (got_taps, got_gated):
                if isinstance(q, int):
                    before = jnp.zeros((rows, rows), f32)
                else:
                    before = turned(source, at, jnp.maximum(q * group - 1, 0))
                    before = jnp.where(q == 0, 0.0, before)
                parts = []
                for e in range(group):
                    now = turned(source, at, q * group + e)
                    parts.append(jnp.where(keep, now, before).astype(bf16))
                    before = now
                matrices.append(jnp.concatenate(parts, axis=0))
            table = jnp.concatenate(matrices, axis=1)
            lines = jnp.concatenate(
                [
                    jnp.concatenate(
                        [pad[pl.ds(n - q * group - e, n), :] for e in range(group)], axis=1
                    ).astype(bf16)
                    for pad in (pad_gated, pad_back)
                ],
                axis=0,
            )
            return total + jnp.dot(lines, table, preferred_element_type=f32)

        sums = jnp.zeros((2 * n, 2 * rows), f32)
        if n == group:
            sums = some_lags(0, sums)
        else:
            sums = lax.fori_loop(0, n // group, some_lags, sums)
        made_mixed[spot, :] = sums[:n, :rows]
        made_conv[spot, :] = sums[n:, :rows]
        made_taps[spot, :] = sums[n:, rows:]

    for h in range(HALVES):
        exchange_wait(TAPS, h)
        exchange_wait(FORTH, h)

        @pl.loop(0, cph)
        def _(c):
            channel(h * slim + c)

        exchange_start(home(h))
        exchange_start(home_last(h))

    for source, target, place in (
        (made_mixed, home_mixed, me),
        (made_conv, home_conv, n - 1 - me),
        (made_taps, home_taps, n - 1 - me),
    ):
        slot(target, me, HALVES * slim)[...] = slot(source, place, HALVES * slim)[...]

    def turn_columns(index):
        for s in range(TEAM):
            left[pl.ds(pl.multiple_of(index * block, 16), block), s * rows : (s + 1) * rows] = (
                slot(got_cols, s * teams + index, rows)[...].T.astype(bf16)
            )

    def held(part, member):
        return slot(proj_all, part * TEAM + member, rows)

    def span_of(part):
        first = (part % KINDS) * channels + (part // KINDS) * width
        return slice(first, first + width)

    def make_values(h):
        exchange_wait(HOME, h)
        conv = reverse(gather(home_conv, h)).T * scaling
        mixed = gather(home_mixed, h).T * scaling
        span = slice(h * width, (h + 1) * width)
        for kind, values in enumerate((
            grad_ref[:, span].astype(f32) * mixed,
            conv * value_rows[:, span],
            conv * key_rows[:, span],
        )):
            held(h * KINDS + kind, mine)[...] = values.astype(bf16).astype(f32)

    side = chip + 1 - 2 * lax.rem(chip, 2)
    pair = lax.rem(chip + 2, CHIPS)
    corner = lax.rem(side + 2, CHIPS)

    def spread_copy(part, k):
        member, target = (
            (mine, pair * 2 + core),
            (mine, side * 2 + core),
            (mine, sibling),
            (pair * 2 + core, side * 2 + core),
            (pair * 2 + core, sibling),
            (side * 2 + core, sibling),
            (corner * 2 + core, sibling),
        )[k]
        return remote(held(part, member), held(part, member), sent_sems.at[SPREAD, 0],
                      recv_sems.at[part, (0, 1, 3, 2, 3, 3, 3)[k]], base + target)

    def arrived(part, k):
        blocks = TEAM // 2 if k == 3 else 1
        region(proj_all, blocks * rows, sent_sems.at[SPREAD, 0], recv_sems.at[part, k]).wait_recv()

    def spread_first(part):
        for k in range(3):
            spread_copy(part, k).start()

    def spread_second(part):
        arrived(part, 0)
        spread_copy(part, 3).start()
        spread_copy(part, 4).start()
        arrived(part, 1)
        spread_copy(part, 5).start()

    def spread_third(part):
        arrived(part, 2)
        spread_copy(part, 6).start()
        arrived(part, 3)

    def sums_copy(part, to_team, from_team, peer):
        return remote(slot(made, part * teams + to_team, block),
                      slot(got, part * teams + from_team, block),
                      sent_sems.at[SUMS, 0], recv_sum_sems.at[part],
                      peer * TEAM + mine)

    def product(part, index):
        lines = left[pl.ds(pl.multiple_of(index * block, 16), block), :]
        right = proj_all[part * TEAM * rows : (part + 1) * TEAM * rows, :].astype(bf16)
        return jnp.dot(lines, right, preferred_element_type=f32)

    def send_products(part):
        @pl.loop(1, teams)
        def _(o):
            target = lax.rem(team + o, teams)
            slot(made, part * teams + target, block)[...] = product(part, target)
            sums_copy(part, target, team, target).start()

    cols_wait(0)

    @pl.loop(1, teams)
    def _(t):
        turn_columns(lax.rem(team + t, teams))

    for h in range(HALVES):
        make_values(h)
        if h == 0:
            spread_first(0)
            spread_first(1)
    for part in range(PARTS + 1):
        if part < PARTS:
            spread_second(part)
            if part + 2 < PARTS:
                spread_first(part + 2)
        if part == KINDS + 1:
            cols_start(1)
        if part > 0:
            spread_third(part - 1)
            send_products(part - 1)

    cols_wait(1)
    turn_columns(team)
    for part in range(PARTS):
        out_ref[:, span_of(part)] = product(part, team)

    tile = min(512, depth)
    lines = jnp.concatenate(
        [
            held(h * KINDS + kind, mine)[...].astype(bf16)
            for kind in range(KINDS)
            for h in range(HALVES)
        ],
        axis=1,
    )

    @pl.loop(0, depth // tile)
    def _(t):
        start = pl.multiple_of(t * tile, tile)
        grad_inputs_ref[:, pl.ds(start, tile)] = lax.dot_general(
            lines, weights[pl.ds(start, tile), :], (((1,), (1,)), ((), ())),
            preferred_element_type=f32,
        ).astype(bf16)

    for h in range(HALVES):
        exchange_wait(LAST, h)
        grad_taps_ref[:, h * width : (h + 1) * width] = reverse(gather(home_taps, h)).T * scaling

    for kind in (TAPS, FORTH, HOME, LAST):
        exchange_sent(kind)
    region(got_cols, (TEAM - 1) * teams * rows, sent_sems.at[COLUMNS, 0],
           recv_cols_sems.at[0]).wait_send()
    region(proj_all, PARTS * 7 * rows, sent_sems.at[SPREAD, 0], recv_sems.at[0, 0]).wait_send()

    for part in range(PARTS):
        span = span_of(part)
        region(got, (teams - 1) * block, sent_sems.at[SUMS, 0], recv_sum_sems.at[part]).wait_recv()

        @pl.loop(1, teams)
        def _(o):
            other = lax.rem(team + o, teams)
            out_ref[:, span] = out_ref[:, span] + slot(got, part * teams + other, block)[...]

        out_ref[:, span] = out_ref[:, span] * scaling

    region(got, PARTS * (teams - 1) * block, sent_sems.at[SUMS, 0], recv_sum_sems.at[0]).wait_send()


def write_kernel(*refs):
    sems = refs[-1]
    copies = [pltpu.make_async_copy(refs[k], refs[3 + k], sems.at[k]) for k in range(3)]
    for copy in copies:
        copy.start()
    for copy in copies:
        copy.wait()


def per_device(inputs, in_weight, filter_taps, grad_out):
    rows, depth = inputs.shape
    channels = filter_taps.shape[1]
    n = lax.axis_size("seq")
    teams = n // TEAM
    scaling = 1.0 / math.sqrt(rows * n)
    width = channels // HALVES
    slim = round_up(width // n, 8)
    block = depth // n
    f32, bf16 = jnp.float32, jnp.bfloat16
    vmem = pl.BlockSpec(memory_space=pltpu.VMEM)
    anywhere = pl.BlockSpec(memory_space=pl.ANY)
    dma = pltpu.SemaphoreType.DMA
    results = pl.pallas_call(
        functools.partial(fused_kernel, n, scaling),
        out_shape=(
            pltpu.VMEM((rows, depth), bf16),
            pltpu.VMEM((block, KINDS * channels), f32),
            pltpu.VMEM((rows, channels), f32),
        ),
        in_specs=[anywhere] * 4,
        out_specs=(vmem,) * 3,
        scratch_shapes=[
            pltpu.VMEM(inputs.shape, inputs.dtype),
            pltpu.VMEM(in_weight.shape, in_weight.dtype),
            pltpu.VMEM(filter_taps.shape, filter_taps.dtype),
            pltpu.VMEM(grad_out.shape, grad_out.dtype),
        ]
        + [pltpu.VMEM((n * HALVES * slim, rows), f32)] * 12
        + [
            pltpu.VMEM((2 * n, rows), f32),
            pltpu.VMEM((2 * n, rows), f32),
            pltpu.VMEM((n * rows, block), f32),
            pltpu.VMEM((n * rows, block), f32),
            pltpu.VMEM((teams * block, TEAM * rows), bf16),
            pltpu.VMEM((rows, channels), f32),
            pltpu.VMEM((rows, channels), f32),
            pltpu.VMEM((PARTS * TEAM * rows, width), f32),
            pltpu.VMEM((PARTS * teams * block, width), f32),
            pltpu.VMEM((PARTS * teams * block, width), f32),
            dma((3,)), dma((PIECES,)), dma((7, HALVES)), dma((4, HALVES)), dma((2,)),
            dma((PARTS, 4)), dma((PARTS,)),
        ],
        compiler_params=pltpu.CompilerParams(
            collective_id=0, has_side_effects=True, vmem_limit_bytes=117 << 19
        ),
    )(inputs, in_weight, filter_taps, grad_out)
    return pl.pallas_call(
        write_kernel,
        out_shape=tuple(jax.ShapeDtypeStruct(r.shape, r.dtype) for r in results),
        in_specs=[anywhere] * 3,
        out_specs=(anywhere,) * 3,
        scratch_shapes=[dma((3,))],
        compiler_params=pltpu.CompilerParams(vmem_limit_bytes=2 << 20),
    )(*results)


def solution(mesh):
    in_specs = (P(("grp", "seq"), None), P(), P("seq", None), P(("grp", "seq"), None))
    out_specs = (P(("grp", "seq"), None), P(("grp", "seq"), None), P(("grp", "seq"), None))
    return jax.shard_map(
        per_device, mesh=mesh, in_specs=in_specs, out_specs=out_specs, check_vma=False
    )
```

```python
import functools
import math

import jax
import jax.numpy as jnp
from jax import lax
from jax.experimental import pallas as pl
from jax.experimental.pallas import tpu as pltpu
from jax.sharding import PartitionSpec as P

GROUP = 16
TEAM = 8
CHIPS = 4
HALVES = 2
KINDS = 3
PARTS = HALVES * KINDS
PIECES = 4
SOON, REST = (3, 1), (0, 2, 4, 5, 6)
TAPS, FORTH, HOME, LAST, COLUMNS, SPREAD, SUMS = range(7)


def round_up(value, step):
    return (value + step - 1) // step * step


def rounds_of(channels, n):
    return 4 if channels // n % 4 == 0 else HALVES


def remote(src, dst, send_sem, recv_sem, peer):
    return pltpu.make_async_remote_copy(
        src_ref=src,
        dst_ref=dst,
        send_sem=send_sem,
        recv_sem=recv_sem,
        device_id={"seq": peer},
        device_id_type=pl.DeviceIdType.MESH,
    )


def fused_kernel(
    n, scaling, x_hbm, weight_hbm, taps_hbm, grad_hbm,
    grad_inputs_ref, out_ref, grad_taps_ref,
    x_ref, weights, taps_ref, grad_ref,
    send_taps, send_pair, got_taps, got_pair, made_pair, made_taps, home_pair, home_taps,
    pad_gated, pad_back, send_cols, got_cols, left, key_rows, value_rows,
    proj_all, made, got,
    load_sems, weight_sems, sent_sems, come_sems, recv_cols_sems, recv_sems, recv_sum_sems,
):
    f32, bf16 = jnp.float32, jnp.bfloat16
    me = lax.axis_index("seq")
    rows, depth = x_ref.shape
    channels = taps_ref.shape[1]
    width = channels // HALVES
    rounds = rounds_of(channels, n)
    few = channels // rounds
    cpr = few // n
    per_half = rounds // HALVES
    slim = round_up(cpr * per_half, 8)
    pair_slim = round_up(2 * cpr, 8)
    teams = n // TEAM
    team, mine = me // TEAM, lax.rem(me, TEAM)
    base, chip, core = team * TEAM, mine // 2, lax.rem(mine, 2)
    sibling = chip * 2 + 1 - core
    block = depth // n
    piece = depth // PIECES

    def slot(ref, index, height):
        return ref.at[pl.ds(pl.multiple_of(index * height, 8), height), :]

    def cell(ref, index, half):
        return slot(ref, index * HALVES + half, slim)

    def pair_cell(ref, index, r):
        return slot(ref, index * rounds + r, pair_slim)

    def load(k):
        span = pl.ds(k * piece, piece)
        return pltpu.make_async_copy(
            weight_hbm.at[span, :], weights.at[span, :], weight_sems.at[k]
        )

    barrier = pltpu.get_barrier_semaphore()

    @pl.loop(1, n)
    def _(o):
        pl.semaphore_signal(
            barrier, inc=1, device_id={"seq": lax.rem(me + o, n)},
            device_id_type=pl.DeviceIdType.MESH,
        )

    load_taps = pltpu.make_async_copy(taps_hbm, taps_ref, load_sems.at[0])
    load_x = pltpu.make_async_copy(x_hbm, x_ref, load_sems.at[1])
    load_grad = pltpu.make_async_copy(grad_hbm, grad_ref, load_sems.at[2])
    load_taps.start()
    load_x.start()
    load_grad.start()
    for k in range(PIECES):
        load(k).start()

    def taps_place(p, r):
        return (p * HALVES + r // per_half) * slim + r % per_half * cpr

    def pair_place(p, r, which):
        return (p * rounds + r) * pair_slim + which * cpr

    def spread(ref, values, place):
        for r in range(rounds):
            for p in range(n):
                at, first = place(p, r), r * few + p * cpr
                ref[at : at + cpr, :] = values[first : first + cpr, :]

    def gather(ref, place):
        return jnp.concatenate([ref[place(p) : place(p) + cpr, :] for p in range(n)], axis=0)

    anti = (
        lax.broadcasted_iota(jnp.int32, (rows, rows), 0)
        + lax.broadcasted_iota(jnp.int32, (rows, rows), 1)
        == rows - 1
    ).astype(f32)

    def reverse(values):
        return jnp.dot(
            values, anti, preferred_element_type=f32, precision=lax.Precision.HIGHEST
        )

    def taps_copy(h):
        def plan(peer, sender):
            return (remote(cell(send_taps, peer, h), cell(got_taps, sender, h),
                           sent_sems.at[TAPS, h], come_sems.at[TAPS, h], peer),)
        return plan

    def forth(r):
        def plan(peer, sender):
            return (remote(pair_cell(send_pair, peer, r), pair_cell(got_pair, sender, r),
                           sent_sems.at[FORTH, r], come_sems.at[FORTH, r], peer),)
        return plan

    def home(r):
        def plan(peer, sender):
            return (remote(pair_cell(made_pair, peer, r), pair_cell(home_pair, sender, r),
                           sent_sems.at[HOME, r], come_sems.at[HOME, r], peer),)
        return plan

    def home_last(h):
        def plan(peer, sender):
            return (remote(cell(made_taps, peer, h), cell(home_taps, sender, h),
                           sent_sems.at[LAST, h], come_sems.at[LAST, h], peer),)
        return plan

    def region(ref, height, send_sem, recv_sem):
        return remote(ref.at[pl.ds(0, height), :], ref.at[pl.ds(0, height), :],
                      send_sem, recv_sem, base + sibling)

    def exchange_start(plan):
        @pl.loop(1, n)
        def _(k):
            o = n - k
            peer = lax.rem(team + o // TEAM, teams) * TEAM + lax.rem(mine + o, TEAM)
            for copy in plan(peer, me):
                copy.start()

    def exchanged(kind, k):
        ref, height = (got_pair, pair_slim) if kind in (FORTH, HOME) else (got_taps, slim)
        return region(ref, (n - 1) * height, sent_sems.at[kind, k], come_sems.at[kind, k])

    def exchange_wait(kind, k):
        exchanged(kind, k).wait_recv()

    def exchange_sent(kind):
        for k in range(rounds if kind in (FORTH, HOME) else HALVES):
            exchanged(kind, k).wait_send()

    def cols(peer, index, sender, late):
        return remote(slot(send_cols, peer * teams + index, rows),
                      slot(got_cols, sender * teams + index, rows),
                      sent_sems.at[COLUMNS, 0], recv_cols_sems.at[late], base + peer)

    side = chip + 1 - 2 * lax.rem(chip, 2)
    pair = lax.rem(chip + 2, CHIPS)
    corner = lax.rem(side + 2, CHIPS)
    peers = (
        sibling,
        side * 2 + core, side * 2 + 1 - core,
        pair * 2 + core, pair * 2 + 1 - core,
        corner * 2 + core, corner * 2 + 1 - core,
    )

    def cols_start(late, chosen):
        @pl.loop(0 if late else 1, 1 if late else teams)
        def _(t):
            for k in chosen:
                cols(peers[k], lax.rem(team + t, teams), mine, late).start()

    def cols_wait(late):
        blocks = (TEAM - 1) * (1 if late else teams - 1)
        region(got_cols, blocks * rows, sent_sems.at[COLUMNS, 0], recv_cols_sems.at[late]).wait_recv()

    load_taps.wait()
    spread(send_taps, taps_ref[...].T, taps_place)
    load_x.wait()
    for g in range(TEAM):
        for t in range(teams):
            first = (t * TEAM + g) * block
            at = (g * teams + t) * rows
            send_cols[at : at + rows, :] = x_ref[:, first : first + block].astype(f32)
    pl.semaphore_wait(barrier, n - 1)
    exchange_start(taps_copy(0))
    cols_start(0, SOON)
    total = jnp.zeros((rows, KINDS * channels), f32)
    for k in range(PIECES):
        load(k).wait()
        total = total + jnp.dot(
            x_ref[:, k * piece : (k + 1) * piece], weights[k * piece : (k + 1) * piece, :],
            preferred_element_type=f32,
        )
    total = total.astype(bf16).astype(f32)
    load_grad.wait()
    spread(
        send_pair, (total[:, channels : 2 * channels] * total[:, 2 * channels :]).T,
        lambda p, r: pair_place(p, r, 0),
    )
    spread(
        send_pair, reverse((grad_ref[...].astype(f32) * total[:, :channels]).T),
        lambda p, r: pair_place(p, r, 1),
    )
    for r in range(rounds):
        if r > 0 and r % per_half == 0:
            exchange_start(taps_copy(r // per_half))
        exchange_start(forth(r))
    key_rows[...] = total[:, channels : 2 * channels]
    value_rows[...] = total[:, 2 * channels :]

    slot(got_cols, mine, teams * rows)[...] = slot(send_cols, mine, teams * rows)[...]
    slot(got_taps, me, HALVES * slim)[...] = slot(send_taps, me, HALVES * slim)[...]
    slot(got_pair, me, rounds * pair_slim)[...] = slot(send_pair, me, rounds * pair_slim)[...]
    pad_gated[pl.ds(0, n), :] = jnp.zeros((n, rows), f32)
    pad_back[pl.ds(n, n), :] = jnp.zeros((n, rows), f32)

    lane = lax.broadcasted_iota(jnp.int32, (rows, rows), 1)
    line = lax.broadcasted_iota(jnp.int32, (rows, rows), 0)
    keep = lane >= line
    group = min(GROUP, n)

    def turned(source, at, step, index):
        row = source[pl.ds(index * step + at, 1), :]
        return pltpu.roll(
            jnp.broadcast_to(row, (rows, rows)), 0, 1, stride=1, stride_axis=0
        )

    def channel(r, c):
        step = rounds * pair_slim
        at = r * pair_slim + c
        at_taps = r // per_half * slim + r % per_half * cpr + c
        here, there = pl.ds(at, n, stride=step), pl.ds(at + cpr, n, stride=step)
        pad_gated[pl.ds(n, n), :] = got_pair[here, :]
        pad_back[pl.ds(0, n), :] = got_pair[there, :]

        def some_lags(q, total):
            matrices = []
            for source, first, jump in ((got_taps, at_taps, HALVES * slim), (got_pair, at, step)):
                if isinstance(q, int):
                    before = jnp.zeros((rows, rows), f32)
                else:
                    before = turned(source, first, jump, jnp.maximum(q * group - 1, 0))
                    before = jnp.where(q == 0, 0.0, before)
                parts = []
                for e in range(group):
                    now = turned(source, first, jump, q * group + e)
                    parts.append(jnp.where(keep, now, before).astype(bf16))
                    before = now
                matrices.append(jnp.concatenate(parts, axis=0))
            table = jnp.concatenate(matrices, axis=1)
            lines = jnp.concatenate(
                [
                    jnp.concatenate(
                        [ref[pl.ds(first + sign * (q * group + e), n), :] for e in range(group)],
                        axis=1,
                    ).astype(bf16)
                    for ref, first, sign in ((pad_gated, n, -1), (pad_back, 0, 1))
                ],
                axis=0,
            )
            return total + jnp.dot(lines, table, preferred_element_type=f32)

        sums = jnp.zeros((2 * n, 2 * rows), f32)
        if n == group:
            sums = some_lags(0, sums)
        else:
            sums = lax.fori_loop(0, n // group, some_lags, sums)
        made_pair[here, :] = sums[:n, :rows]
        made_pair[there, :] = sums[n:, :rows]
        made_taps[pl.ds(at_taps, n, stride=HALVES * slim), :] = sums[n:, rows:]

    def convolve(r):
        if r % per_half == 0:
            exchange_wait(TAPS, r // per_half)
        exchange_wait(FORTH, r)

        @pl.loop(0, cpr)
        def _(c):
            channel(r, c)

        exchange_start(home(r))
        if (r + 1) % per_half == 0:
            h = r // per_half
            exchange_start(home_last(h))
            cell(home_taps, me, h)[...] = cell(made_taps, me, h)[...]
        pair_cell(home_pair, me, r)[...] = pair_cell(made_pair, me, r)[...]

    def turn_columns(index):
        for s in range(TEAM):
            left[pl.ds(pl.multiple_of(index * block, 16), block), s * rows : (s + 1) * rows] = (
                slot(got_cols, s * teams + index, rows)[...].T.astype(bf16)
            )

    def held(part, member):
        return slot(proj_all, part * TEAM + member, rows)

    chunks = rounds * KINDS // PARTS

    def spans_of(part):
        spans = []
        for j in range(chunks):
            r, kind = divmod(part * chunks + j, KINDS)
            spans.append((slice(j * few, (j + 1) * few), kind * channels + r * few))
        return [(inside, slice(first, first + few)) for inside, first in spans]

    def make_values(r):
        exchange_wait(HOME, r)
        conv = reverse(gather(home_pair, lambda p: pair_place(p, r, 1))).T * scaling
        mixed = gather(home_pair, lambda p: pair_place(p, r, 0)).T * scaling
        span = slice(r * few, (r + 1) * few)
        for kind, values in enumerate((
            grad_ref[:, span].astype(f32) * mixed,
            conv * value_rows[:, span],
            conv * key_rows[:, span],
        )):
            part, j = divmod(r * KINDS + kind, chunks)
            held(part, mine)[:, j * few : (j + 1) * few] = values.astype(bf16).astype(f32)

    def spread_copy(part, k):
        member, target = (
            (mine, pair * 2 + core),
            (mine, side * 2 + core),
            (mine, sibling),
            (pair * 2 + core, side * 2 + core),
            (pair * 2 + core, sibling),
            (side * 2 + core, sibling),
            (corner * 2 + core, sibling),
        )[k]
        return remote(held(part, member), held(part, member), sent_sems.at[SPREAD, 0],
                      recv_sems.at[part, (0, 1, 3, 2, 3, 3, 3)[k]], base + target)

    def arrived(part, k):
        blocks = TEAM // 2 if k == 3 else 1
        region(proj_all, blocks * rows, sent_sems.at[SPREAD, 0], recv_sems.at[part, k]).wait_recv()

    def spread_first(part):
        for k in range(3):
            spread_copy(part, k).start()

    def spread_second(part):
        arrived(part, 0)
        spread_copy(part, 3).start()
        spread_copy(part, 4).start()
        arrived(part, 1)
        spread_copy(part, 5).start()

    def spread_third(part):
        arrived(part, 2)
        spread_copy(part, 6).start()
        arrived(part, 3)

    def sums_copy(part, to_team, from_team, peer):
        return remote(slot(made, part * teams + to_team, block),
                      slot(got, part * teams + from_team, block),
                      sent_sems.at[SUMS, 0], recv_sum_sems.at[part],
                      peer * TEAM + mine)

    def product(part, index):
        lines = left[pl.ds(pl.multiple_of(index * block, 16), block), :]
        right = proj_all[part * TEAM * rows : (part + 1) * TEAM * rows, :].astype(bf16)
        return jnp.dot(lines, right, preferred_element_type=f32)

    def send_products(part):
        @pl.loop(1, teams)
        def _(o):
            target = lax.rem(team + o, teams)
            slot(made, part * teams + target, block)[...] = product(part, target)
            sums_copy(part, target, team, target).start()

    def first_columns(chosen):
        cols_start(0, chosen)

    def late_columns(chosen):
        cols_start(1, chosen)

    def turn_first(_):
        cols_wait(0)

        @pl.loop(1, teams)
        def _(t):
            turn_columns(lax.rem(team + t, teams))

    if rounds == 4:
        steps = (
            (first_columns, (4, 2, 5)), (convolve, 0), (first_columns, (6, 0)), (convolve, 1),
            (make_values, 0), (spread_first, 0), (convolve, 2), (make_values, 1),
            (spread_second, 0), (spread_first, 1), (spread_first, 2), (convolve, 3),
            (make_values, 2), (spread_first, 3), (spread_second, 1), (turn_first, 0),
            (spread_third, 0), (send_products, 0), (late_columns, (3, 1)), (spread_second, 2),
            (spread_third, 1), (send_products, 1), (late_columns, (4, 2)), (make_values, 3),
            (spread_first, 4), (spread_first, 5), (spread_second, 3), (spread_third, 2),
            (send_products, 2), (late_columns, (5, 0)), (spread_second, 4), (spread_third, 3),
            (send_products, 3), (late_columns, (6,)), (spread_second, 5), (spread_third, 4),
            (send_products, 4), (spread_third, 5), (send_products, 5),
        )
    else:
        steps = (
            [(first_columns, REST)]
            + [(convolve, r) for r in range(rounds)]
            + [(make_values, r) for r in range(rounds)]
            + [(spread_first, p) for p in range(PARTS)]
            + [(turn_first, 0), (late_columns, SOON + REST)]
            + [(act, p) for p in range(PARTS) for act in (spread_second, spread_third, send_products)]
        )
    for act, given in steps:
        act(given)

    tile = min(512, depth)
    lines = jnp.concatenate(
        [
            held((r * KINDS + kind) // chunks, mine)[
                :, (r * KINDS + kind) % chunks * few : ((r * KINDS + kind) % chunks + 1) * few
            ].astype(bf16)
            for kind in range(KINDS)
            for r in range(rounds)
        ],
        axis=1,
    )

    @pl.loop(0, depth // tile)
    def _(t):
        start = pl.multiple_of(t * tile, tile)
        grad_inputs_ref[:, pl.ds(start, tile)] = lax.dot_general(
            lines, weights[pl.ds(start, tile), :], (((1,), (1,)), ((), ())),
            preferred_element_type=f32,
        ).astype(bf16)

    for h in range(HALVES):
        exchange_wait(LAST, h)
    for r in range(rounds):
        grad_taps_ref[:, r * few : (r + 1) * few] = (
            reverse(gather(home_taps, lambda p: taps_place(p, r))).T * scaling
        )

    cols_wait(1)
    turn_columns(team)
    for part in range(PARTS):
        made_here = product(part, team)
        for inside, span in spans_of(part):
            out_ref[:, span] = made_here[:, inside]

    for kind in (TAPS, FORTH, HOME, LAST):
        exchange_sent(kind)
    region(got_cols, (TEAM - 1) * teams * rows, sent_sems.at[COLUMNS, 0],
           recv_cols_sems.at[0]).wait_send()
    region(proj_all, PARTS * 7 * rows, sent_sems.at[SPREAD, 0], recv_sems.at[0, 0]).wait_send()

    for part in range(PARTS):
        region(got, (teams - 1) * block, sent_sems.at[SUMS, 0], recv_sum_sems.at[part]).wait_recv()

        for inside, span in spans_of(part):
            kept = out_ref[:, span]
            if teams == 2:
                kept = kept + slot(got, part * teams + 1 - team, block)[:, inside]
            else:
                def add_one(o, kept):
                    other = lax.rem(team + o, teams)
                    return kept + slot(got, part * teams + other, block)[:, inside]

                kept = lax.fori_loop(1, teams, add_one, kept)
            out_ref[:, span] = kept * scaling

    region(got, PARTS * (teams - 1) * block, sent_sems.at[SUMS, 0], recv_sum_sems.at[0]).wait_send()


def write_kernel(*refs):
    sems = refs[-1]
    copies = [pltpu.make_async_copy(refs[k], refs[3 + k], sems.at[k]) for k in range(3)]
    for copy in copies:
        copy.start()
    for copy in copies:
        copy.wait()


def per_device(inputs, in_weight, filter_taps, grad_out):
    rows, depth = inputs.shape
    channels = filter_taps.shape[1]
    n = lax.axis_size("seq")
    teams = n // TEAM
    scaling = 1.0 / math.sqrt(rows * n)
    width = channels // HALVES
    rounds = rounds_of(channels, n)
    cpr = channels // rounds // n
    slim = round_up(cpr * (rounds // HALVES), 8)
    pair_slim = round_up(2 * cpr, 8)
    half, whole = n * HALVES * slim, n * rounds * pair_slim
    block = depth // n
    f32, bf16 = jnp.float32, jnp.bfloat16
    vmem = pl.BlockSpec(memory_space=pltpu.VMEM)
    anywhere = pl.BlockSpec(memory_space=pl.ANY)
    dma = pltpu.SemaphoreType.DMA
    results = pl.pallas_call(
        functools.partial(fused_kernel, n, scaling),
        out_shape=(
            pltpu.VMEM((rows, depth), bf16),
            pltpu.VMEM((block, KINDS * channels), f32),
            pltpu.VMEM((rows, channels), f32),
        ),
        in_specs=[anywhere] * 4,
        out_specs=(vmem,) * 3,
        scratch_shapes=[
            pltpu.VMEM(inputs.shape, inputs.dtype),
            pltpu.VMEM(in_weight.shape, in_weight.dtype),
            pltpu.VMEM(filter_taps.shape, filter_taps.dtype),
            pltpu.VMEM(grad_out.shape, grad_out.dtype),
        ]
        + [
            pltpu.VMEM((height, rows), f32)
            for height in (half, whole, half, whole, whole, half, whole, half)
        ]
        + [
            pltpu.VMEM((2 * n, rows), f32),
            pltpu.VMEM((2 * n, rows), f32),
            pltpu.VMEM((n * rows, block), f32),
            pltpu.VMEM((n * rows, block), f32),
            pltpu.VMEM((teams * block, TEAM * rows), bf16),
            pltpu.VMEM((rows, channels), f32),
            pltpu.VMEM((rows, channels), f32),
            pltpu.VMEM((PARTS * TEAM * rows, width), f32),
            pltpu.VMEM((PARTS * teams * block, width), f32),
            pltpu.VMEM((PARTS * teams * block, width), f32),
            dma((3,)), dma((PIECES,)), dma((7, rounds)), dma((4, rounds)), dma((2,)),
            dma((PARTS, 4)), dma((PARTS,)),
        ],
        compiler_params=pltpu.CompilerParams(
            collective_id=0, has_side_effects=True, vmem_limit_bytes=117 << 19
        ),
    )(inputs, in_weight, filter_taps, grad_out)
    return pl.pallas_call(
        write_kernel,
        out_shape=tuple(jax.ShapeDtypeStruct(r.shape, r.dtype) for r in results),
        in_specs=[anywhere] * 3,
        out_specs=(anywhere,) * 3,
        scratch_shapes=[dma((3,))],
        compiler_params=pltpu.CompilerParams(vmem_limit_bytes=2 << 20),
    )(*results)


def solution(mesh):
    in_specs = (P(("grp", "seq"), None), P(), P("seq", None), P(("grp", "seq"), None))
    out_specs = (P(("grp", "seq"), None), P(("grp", "seq"), None), P(("grp", "seq"), None))
    return jax.shard_map(
        per_device, mesh=mesh, in_specs=in_specs, out_specs=out_specs, check_vma=False
    )
```

```python
import functools
import math

import jax
import jax.numpy as jnp
from jax import lax
from jax.experimental import pallas as pl
from jax.experimental.pallas import tpu as pltpu
from jax.sharding import PartitionSpec as P

GROUP = 16
TEAM = 8
CHIPS = 4
HALVES = 2
KINDS = 3
PARTS = HALVES * KINDS
PIECES = 4
SOON, REST = (3, 1), (0, 2, 4, 5, 6)
TAPS, FORTH, HOME, LAST, COLUMNS, SPREAD, SUMS = range(7)


def round_up(value, step):
    return (value + step - 1) // step * step


def rounds_of(channels, n):
    return 4 if channels // n % 4 == 0 else HALVES


def remote(src, dst, send_sem, recv_sem, peer):
    return pltpu.make_async_remote_copy(
        src_ref=src,
        dst_ref=dst,
        send_sem=send_sem,
        recv_sem=recv_sem,
        device_id={"seq": peer},
        device_id_type=pl.DeviceIdType.MESH,
    )


def fused_kernel(
    n, scaling, x_hbm, weight_hbm, taps_hbm, grad_hbm,
    grad_inputs_ref, out_ref, grad_taps_ref,
    x_ref, weights, taps_ref, grad_ref,
    send_taps, send_pair, got_taps, got_pair, made_pair, made_taps, home_pair, home_taps,
    pad_gated, pad_back, send_cols, got_cols, left, key_rows, value_rows,
    proj_all, made, got,
    load_sems, weight_sems, sent_sems, come_sems, recv_cols_sems, recv_sems, recv_sum_sems,
):
    f32, bf16 = jnp.float32, jnp.bfloat16
    me = lax.axis_index("seq")
    rows, depth = x_ref.shape
    channels = taps_ref.shape[1]
    width = channels // HALVES
    rounds = rounds_of(channels, n)
    few = channels // rounds
    cpr = few // n
    per_half = rounds // HALVES
    slim = round_up(cpr * per_half, 8)
    pair_slim = round_up(2 * cpr, 8)
    teams = n // TEAM
    team, mine = me // TEAM, lax.rem(me, TEAM)
    base, chip, core = team * TEAM, mine // 2, lax.rem(mine, 2)
    sibling = chip * 2 + 1 - core
    block = depth // n
    piece = depth // PIECES

    def slot(ref, index, height):
        return ref.at[pl.ds(pl.multiple_of(index * height, 8), height), :]

    def cell(ref, index, half):
        return slot(ref, index * HALVES + half, slim)

    def pair_cell(ref, index, r):
        return slot(ref, index * rounds + r, pair_slim)

    def load(k):
        span = pl.ds(k * piece, piece)
        return pltpu.make_async_copy(
            weight_hbm.at[span, :], weights.at[span, :], weight_sems.at[k]
        )

    barrier = pltpu.get_barrier_semaphore()

    @pl.loop(1, n)
    def _(o):
        pl.semaphore_signal(
            barrier, inc=1, device_id={"seq": lax.rem(me + o, n)},
            device_id_type=pl.DeviceIdType.MESH,
        )

    load_taps = pltpu.make_async_copy(taps_hbm, taps_ref, load_sems.at[0])
    load_x = pltpu.make_async_copy(x_hbm, x_ref, load_sems.at[1])
    load_grad = pltpu.make_async_copy(grad_hbm, grad_ref, load_sems.at[2])
    load_taps.start()
    load_x.start()
    load_grad.start()
    for k in range(PIECES):
        load(k).start()

    def taps_place(p, r):
        return (p * HALVES + r // per_half) * slim + r % per_half * cpr

    def pair_place(p, r, which):
        return (p * rounds + r) * pair_slim + which * cpr

    def spread(ref, values, place):
        for r in range(rounds):
            for p in range(n):
                at, first = place(p, r), r * few + p * cpr
                ref[at : at + cpr, :] = values[first : first + cpr, :]

    def gather(ref, place):
        return jnp.concatenate([ref[place(p) : place(p) + cpr, :] for p in range(n)], axis=0)

    anti = (
        lax.broadcasted_iota(jnp.int32, (rows, rows), 0)
        + lax.broadcasted_iota(jnp.int32, (rows, rows), 1)
        == rows - 1
    ).astype(f32)

    def reverse(values):
        return jnp.dot(
            values, anti, preferred_element_type=f32, precision=lax.Precision.HIGHEST
        )

    def taps_copy(h):
        def plan(peer, sender):
            return (remote(cell(send_taps, peer, h), cell(got_taps, sender, h),
                           sent_sems.at[TAPS, h], come_sems.at[TAPS, h], peer),)
        return plan

    def forth(r):
        def plan(peer, sender):
            return (remote(pair_cell(send_pair, peer, r), pair_cell(got_pair, sender, r),
                           sent_sems.at[FORTH, r], come_sems.at[FORTH, r], peer),)
        return plan

    def home(r):
        def plan(peer, sender):
            return (remote(pair_cell(made_pair, peer, r), pair_cell(home_pair, sender, r),
                           sent_sems.at[HOME, r], come_sems.at[HOME, r], peer),)
        return plan

    def home_last(h):
        def plan(peer, sender):
            return (remote(cell(made_taps, peer, h), cell(home_taps, sender, h),
                           sent_sems.at[LAST, h], come_sems.at[LAST, h], peer),)
        return plan

    def region(ref, height, send_sem, recv_sem):
        return remote(ref.at[pl.ds(0, height), :], ref.at[pl.ds(0, height), :],
                      send_sem, recv_sem, base + sibling)

    def exchange_start(plan):
        @pl.loop(1, n)
        def _(k):
            o = n - k
            peer = lax.rem(team + o // TEAM, teams) * TEAM + lax.rem(mine + o, TEAM)
            for copy in plan(peer, me):
                copy.start()

    def exchanged(kind, k):
        ref, height = (got_pair, pair_slim) if kind in (FORTH, HOME) else (got_taps, slim)
        return region(ref, (n - 1) * height, sent_sems.at[kind, k], come_sems.at[kind, k])

    def exchange_wait(kind, k):
        exchanged(kind, k).wait_recv()

    def exchange_sent(kind):
        for k in range(rounds if kind in (FORTH, HOME) else HALVES):
            exchanged(kind, k).wait_send()

    def cols(peer, index, sender, late):
        return remote(slot(send_cols, peer * teams + index, rows),
                      slot(got_cols, sender * teams + index, rows),
                      sent_sems.at[COLUMNS, 0], recv_cols_sems.at[late], base + peer)

    side = chip + 1 - 2 * lax.rem(chip, 2)
    pair = lax.rem(chip + 2, CHIPS)
    corner = lax.rem(side + 2, CHIPS)
    peers = (
        sibling,
        side * 2 + core, side * 2 + 1 - core,
        pair * 2 + core, pair * 2 + 1 - core,
        corner * 2 + core, corner * 2 + 1 - core,
    )

    def cols_start(late, chosen):
        @pl.loop(0 if late else 1, 1 if late else teams)
        def _(t):
            for k in chosen:
                cols(peers[k], lax.rem(team + t, teams), mine, late).start()

    def cols_wait(late):
        blocks = (TEAM - 1) * (1 if late else teams - 1)
        region(got_cols, blocks * rows, sent_sems.at[COLUMNS, 0], recv_cols_sems.at[late]).wait_recv()

    load_taps.wait()
    spread(send_taps, taps_ref[...].T, taps_place)
    load_x.wait()
    for g in range(TEAM):
        for t in range(teams):
            first = (t * TEAM + g) * block
            at = (g * teams + t) * rows
            send_cols[at : at + rows, :] = x_ref[:, first : first + block].astype(f32)
    pl.semaphore_wait(barrier, n - 1)
    exchange_start(taps_copy(0))
    cols_start(0, SOON)
    total = jnp.zeros((rows, KINDS * channels), f32)
    for k in range(PIECES):
        load(k).wait()
        total = total + jnp.dot(
            x_ref[:, k * piece : (k + 1) * piece], weights[k * piece : (k + 1) * piece, :],
            preferred_element_type=f32,
        )
    total = total.astype(bf16).astype(f32)
    load_grad.wait()
    spread(
        send_pair, (total[:, channels : 2 * channels] * total[:, 2 * channels :]).T,
        lambda p, r: pair_place(p, r, 0),
    )
    spread(
        send_pair, reverse((grad_ref[...].astype(f32) * total[:, :channels]).T),
        lambda p, r: pair_place(p, r, 1),
    )
    for r in range(rounds):
        if r > 0 and r % per_half == 0:
            exchange_start(taps_copy(r // per_half))
        exchange_start(forth(r))
    key_rows[...] = total[:, channels : 2 * channels]
    value_rows[...] = total[:, 2 * channels :]

    slot(got_cols, mine, teams * rows)[...] = slot(send_cols, mine, teams * rows)[...]
    slot(got_taps, me, HALVES * slim)[...] = slot(send_taps, me, HALVES * slim)[...]
    slot(got_pair, me, rounds * pair_slim)[...] = slot(send_pair, me, rounds * pair_slim)[...]
    pad_gated[pl.ds(0, n), :] = jnp.zeros((n, rows), f32)
    pad_back[pl.ds(n, n), :] = jnp.zeros((n, rows), f32)

    lane = lax.broadcasted_iota(jnp.int32, (rows, rows), 1)
    line = lax.broadcasted_iota(jnp.int32, (rows, rows), 0)
    keep = lane >= line
    group = min(GROUP, n)

    def turned(source, at, step, index):
        row = source[pl.ds(index * step + at, 1), :]
        return pltpu.roll(
            jnp.broadcast_to(row, (rows, rows)), 0, 1, stride=1, stride_axis=0
        )

    def channel(r, c):
        step = rounds * pair_slim
        at = r * pair_slim + c
        at_taps = r // per_half * slim + r % per_half * cpr + c
        here, there = pl.ds(at, n, stride=step), pl.ds(at + cpr, n, stride=step)
        pad_gated[pl.ds(n, n), :] = got_pair[here, :]
        pad_back[pl.ds(0, n), :] = got_pair[there, :]

        def some_lags(q, total):
            matrices = []
            for source, first, jump in ((got_taps, at_taps, HALVES * slim), (got_pair, at, step)):
                if isinstance(q, int):
                    before = jnp.zeros((rows, rows), f32)
                else:
                    before = turned(source, first, jump, jnp.maximum(q * group - 1, 0))
                    before = jnp.where(q == 0, 0.0, before)
                parts = []
                for e in range(group):
                    now = turned(source, first, jump, q * group + e)
                    parts.append(jnp.where(keep, now, before).astype(bf16))
                    before = now
                matrices.append(jnp.concatenate(parts, axis=0))
            table = jnp.concatenate(matrices, axis=1)
            lines = jnp.concatenate(
                [
                    jnp.concatenate(
                        [ref[pl.ds(first + sign * (q * group + e), n), :] for e in range(group)],
                        axis=1,
                    ).astype(bf16)
                    for ref, first, sign in ((pad_gated, n, -1), (pad_back, 0, 1))
                ],
                axis=0,
            )
            return total + jnp.dot(lines, table, preferred_element_type=f32)

        sums = jnp.zeros((2 * n, 2 * rows), f32)
        if n == group:
            sums = some_lags(0, sums)
        else:
            sums = lax.fori_loop(0, n // group, some_lags, sums)
        made_pair[here, :] = sums[:n, :rows]
        made_pair[there, :] = sums[n:, :rows]
        made_taps[pl.ds(at_taps, n, stride=HALVES * slim), :] = sums[n:, rows:]

    def convolve(r):
        if r % per_half == 0:
            exchange_wait(TAPS, r // per_half)
        exchange_wait(FORTH, r)

        @pl.loop(0, cpr)
        def _(c):
            channel(r, c)

        exchange_start(home(r))
        if (r + 1) % per_half == 0:
            h = r // per_half
            exchange_start(home_last(h))
            cell(home_taps, me, h)[...] = cell(made_taps, me, h)[...]
        pair_cell(home_pair, me, r)[...] = pair_cell(made_pair, me, r)[...]

    def turn_columns(index):
        for s in range(TEAM):
            left[pl.ds(pl.multiple_of(index * block, 16), block), s * rows : (s + 1) * rows] = (
                slot(got_cols, s * teams + index, rows)[...].T.astype(bf16)
            )

    def held(part, member):
        return slot(proj_all, part * TEAM + member, rows)

    chunks = rounds * KINDS // PARTS

    def spans_of(part):
        spans = []
        for j in range(chunks):
            r, kind = divmod(part * chunks + j, KINDS)
            spans.append((slice(j * few, (j + 1) * few), kind * channels + r * few))
        return [(inside, slice(first, first + few)) for inside, first in spans]

    def make_values(r):
        exchange_wait(HOME, r)
        conv = reverse(gather(home_pair, lambda p: pair_place(p, r, 1))).T * scaling
        mixed = gather(home_pair, lambda p: pair_place(p, r, 0)).T * scaling
        span = slice(r * few, (r + 1) * few)
        for kind, values in enumerate((
            grad_ref[:, span].astype(f32) * mixed,
            conv * value_rows[:, span],
            conv * key_rows[:, span],
        )):
            part, j = divmod(r * KINDS + kind, chunks)
            held(part, mine)[:, j * few : (j + 1) * few] = values.astype(bf16).astype(f32)

    def spread_copy(part, k):
        member, target = (
            (mine, pair * 2 + core),
            (mine, side * 2 + core),
            (mine, sibling),
            (pair * 2 + core, side * 2 + core),
            (pair * 2 + core, sibling),
            (side * 2 + core, sibling),
            (corner * 2 + core, sibling),
        )[k]
        return remote(held(part, member), held(part, member), sent_sems.at[SPREAD, 0],
                      recv_sems.at[part, (0, 1, 3, 2, 3, 3, 3)[k]], base + target)

    def arrived(part, k):
        blocks = TEAM // 2 if k == 3 else 1
        region(proj_all, blocks * rows, sent_sems.at[SPREAD, 0], recv_sems.at[part, k]).wait_recv()

    def spread_first(part):
        for k in range(3):
            spread_copy(part, k).start()

    def spread_second(part):
        arrived(part, 0)
        spread_copy(part, 3).start()
        spread_copy(part, 4).start()
        arrived(part, 1)
        spread_copy(part, 5).start()

    def spread_third(part):
        arrived(part, 2)
        spread_copy(part, 6).start()
        arrived(part, 3)

    def sums_copy(part, to_team, from_team, peer):
        return remote(slot(made, part * teams + to_team, block),
                      slot(got, part * teams + from_team, block),
                      sent_sems.at[SUMS, 0], recv_sum_sems.at[part],
                      peer * TEAM + mine)

    def product(part, index):
        lines = left[pl.ds(pl.multiple_of(index * block, 16), block), :]
        right = proj_all[part * TEAM * rows : (part + 1) * TEAM * rows, :].astype(bf16)
        return jnp.dot(lines, right, preferred_element_type=f32)

    def send_products(part):
        @pl.loop(1, teams)
        def _(o):
            target = lax.rem(team + o, teams)
            slot(made, part * teams + target, block)[...] = product(part, target)
            sums_copy(part, target, team, target).start()

    def first_columns(chosen):
        cols_start(0, chosen)

    def late_columns(chosen):
        cols_start(1, chosen)

    def turn_first(_):
        cols_wait(0)

        @pl.loop(1, teams)
        def _(t):
            turn_columns(lax.rem(team + t, teams))

    if rounds == 4:
        steps = (
            (first_columns, (4, 2)), (convolve, 0), (first_columns, (5,)), (convolve, 1),
            (make_values, 0), (spread_first, 0), (first_columns, (6, 0)), (convolve, 2),
            (make_values, 1), (spread_second, 0), (spread_first, 1), (spread_first, 2),
            (convolve, 3), (make_values, 2), (spread_first, 3), (spread_second, 1),
            (turn_first, 0), (spread_third, 0), (send_products, 0), (late_columns, (3, 1)),
            (spread_second, 2), (spread_third, 1), (send_products, 1), (late_columns, (4, 2)),
            (make_values, 3), (spread_first, 4), (spread_first, 5), (spread_second, 3),
            (spread_third, 2), (send_products, 2), (late_columns, (5, 0)), (spread_second, 4),
            (spread_third, 3), (send_products, 3), (late_columns, (6,)), (spread_second, 5),
            (spread_third, 4), (send_products, 4), (spread_third, 5), (send_products, 5),
        )
    else:
        steps = (
            [(first_columns, REST)]
            + [(convolve, r) for r in range(rounds)]
            + [(make_values, r) for r in range(rounds)]
            + [(spread_first, p) for p in range(PARTS)]
            + [(turn_first, 0), (late_columns, SOON + REST)]
            + [(act, p) for p in range(PARTS) for act in (spread_second, spread_third, send_products)]
        )
    for act, given in steps:
        act(given)

    tile = min(512, depth)
    lines = jnp.concatenate(
        [
            held((r * KINDS + kind) // chunks, mine)[
                :, (r * KINDS + kind) % chunks * few : ((r * KINDS + kind) % chunks + 1) * few
            ].astype(bf16)
            for kind in range(KINDS)
            for r in range(rounds)
        ],
        axis=1,
    )

    @pl.loop(0, depth // tile)
    def _(t):
        start = pl.multiple_of(t * tile, tile)
        grad_inputs_ref[:, pl.ds(start, tile)] = lax.dot_general(
            lines, weights[pl.ds(start, tile), :], (((1,), (1,)), ((), ())),
            preferred_element_type=f32,
        ).astype(bf16)

    for h in range(HALVES):
        exchange_wait(LAST, h)
    for r in range(rounds):
        grad_taps_ref[:, r * few : (r + 1) * few] = (
            reverse(gather(home_taps, lambda p: taps_place(p, r))).T * scaling
        )

    cols_wait(1)
    turn_columns(team)
    for part in range(PARTS):
        made_here = product(part, team)
        for inside, span in spans_of(part):
            out_ref[:, span] = made_here[:, inside]

    for kind in (TAPS, FORTH, HOME, LAST):
        exchange_sent(kind)
    region(got_cols, (TEAM - 1) * teams * rows, sent_sems.at[COLUMNS, 0],
           recv_cols_sems.at[0]).wait_send()
    region(proj_all, PARTS * 7 * rows, sent_sems.at[SPREAD, 0], recv_sems.at[0, 0]).wait_send()

    for part in range(PARTS):
        region(got, (teams - 1) * block, sent_sems.at[SUMS, 0], recv_sum_sems.at[part]).wait_recv()

        for inside, span in spans_of(part):
            kept = out_ref[:, span]
            if teams == 2:
                kept = kept + slot(got, part * teams + 1 - team, block)[:, inside]
            else:
                def add_one(o, kept):
                    other = lax.rem(team + o, teams)
                    return kept + slot(got, part * teams + other, block)[:, inside]

                kept = lax.fori_loop(1, teams, add_one, kept)
            out_ref[:, span] = kept * scaling

    region(got, PARTS * (teams - 1) * block, sent_sems.at[SUMS, 0], recv_sum_sems.at[0]).wait_send()


def write_kernel(*refs):
    sems = refs[-1]
    copies = [pltpu.make_async_copy(refs[k], refs[3 + k], sems.at[k]) for k in range(3)]
    for copy in copies:
        copy.start()
    for copy in copies:
        copy.wait()


def per_device(inputs, in_weight, filter_taps, grad_out):
    rows, depth = inputs.shape
    channels = filter_taps.shape[1]
    n = lax.axis_size("seq")
    teams = n // TEAM
    scaling = 1.0 / math.sqrt(rows * n)
    width = channels // HALVES
    rounds = rounds_of(channels, n)
    cpr = channels // rounds // n
    slim = round_up(cpr * (rounds // HALVES), 8)
    pair_slim = round_up(2 * cpr, 8)
    half, whole = n * HALVES * slim, n * rounds * pair_slim
    block = depth // n
    f32, bf16 = jnp.float32, jnp.bfloat16
    vmem = pl.BlockSpec(memory_space=pltpu.VMEM)
    anywhere = pl.BlockSpec(memory_space=pl.ANY)
    dma = pltpu.SemaphoreType.DMA
    results = pl.pallas_call(
        functools.partial(fused_kernel, n, scaling),
        out_shape=(
            pltpu.VMEM((rows, depth), bf16),
            pltpu.VMEM((block, KINDS * channels), f32),
            pltpu.VMEM((rows, channels), f32),
        ),
        in_specs=[anywhere] * 4,
        out_specs=(vmem,) * 3,
        scratch_shapes=[
            pltpu.VMEM(inputs.shape, inputs.dtype),
            pltpu.VMEM(in_weight.shape, in_weight.dtype),
            pltpu.VMEM(filter_taps.shape, filter_taps.dtype),
            pltpu.VMEM(grad_out.shape, grad_out.dtype),
        ]
        + [
            pltpu.VMEM((height, rows), f32)
            for height in (half, whole, half, whole, whole, half, whole, half)
        ]
        + [
            pltpu.VMEM((2 * n, rows), f32),
            pltpu.VMEM((2 * n, rows), f32),
            pltpu.VMEM((n * rows, block), f32),
            pltpu.VMEM((n * rows, block), f32),
            pltpu.VMEM((teams * block, TEAM * rows), bf16),
            pltpu.VMEM((rows, channels), f32),
            pltpu.VMEM((rows, channels), f32),
            pltpu.VMEM((PARTS * TEAM * rows, width), f32),
            pltpu.VMEM((PARTS * teams * block, width), f32),
            pltpu.VMEM((PARTS * teams * block, width), f32),
            dma((3,)), dma((PIECES,)), dma((7, rounds)), dma((4, rounds)), dma((2,)),
            dma((PARTS, 4)), dma((PARTS,)),
        ],
        compiler_params=pltpu.CompilerParams(
            collective_id=0, has_side_effects=True, vmem_limit_bytes=117 << 19
        ),
    )(inputs, in_weight, filter_taps, grad_out)
    return pl.pallas_call(
        write_kernel,
        out_shape=tuple(jax.ShapeDtypeStruct(r.shape, r.dtype) for r in results),
        in_specs=[anywhere] * 3,
        out_specs=(anywhere,) * 3,
        scratch_shapes=[dma((3,))],
        compiler_params=pltpu.CompilerParams(vmem_limit_bytes=2 << 20),
    )(*results)


def solution(mesh):
    in_specs = (P(("grp", "seq"), None), P(), P("seq", None), P(("grp", "seq"), None))
    out_specs = (P(("grp", "seq"), None), P(("grp", "seq"), None), P(("grp", "seq"), None))
    return jax.shard_map(
        per_device, mesh=mesh, in_specs=in_specs, out_specs=out_specs, check_vma=False
    )
```

```python
import functools
import math

import jax
import jax.numpy as jnp
from jax import lax
from jax.experimental import pallas as pl
from jax.experimental.pallas import tpu as pltpu
from jax.sharding import PartitionSpec as P

GROUP = 16
TEAM = 8
CHIPS = 4
HALVES = 2
KINDS = 3
PARTS = HALVES * KINDS
PIECES = 4
SOON, REST = (3, 1), (0, 2, 4, 5, 6)
TAPS, FORTH, HOME, LAST, COLUMNS, SPREAD, SUMS = range(7)


def round_up(value, step):
    return (value + step - 1) // step * step


def rounds_of(channels, n):
    return 4 if channels // n % 4 == 0 else HALVES


def remote(src, dst, send_sem, recv_sem, peer):
    return pltpu.make_async_remote_copy(
        src_ref=src,
        dst_ref=dst,
        send_sem=send_sem,
        recv_sem=recv_sem,
        device_id={"seq": peer},
        device_id_type=pl.DeviceIdType.MESH,
    )


def fused_kernel(
    n, scaling, x_hbm, weight_hbm, taps_hbm, grad_hbm,
    grad_inputs_ref, out_ref, grad_taps_ref,
    x_ref, weights, taps_ref, grad_ref,
    send_taps, send_pair, got_taps, got_pair, made_pair, made_taps, home_pair, home_taps,
    pad_gated, pad_back, send_cols, got_cols, left, key_rows, value_rows,
    proj_all, made, got,
    load_sems, weight_sems, sent_sems, come_sems, recv_cols_sems, recv_sems, recv_sum_sems,
):
    f32, bf16 = jnp.float32, jnp.bfloat16
    me = lax.axis_index("seq")
    rows, depth = x_ref.shape
    channels = taps_ref.shape[1]
    width = channels // HALVES
    rounds = rounds_of(channels, n)
    few = channels // rounds
    cpr = few // n
    per_half = rounds // HALVES
    slim = round_up(cpr * per_half, 8)
    pair_slim = round_up(2 * cpr, 8)
    teams = n // TEAM
    team, mine = me // TEAM, lax.rem(me, TEAM)
    base, chip, core = team * TEAM, mine // 2, lax.rem(mine, 2)
    sibling = chip * 2 + 1 - core
    block = depth // n
    piece = depth // PIECES

    def slot(ref, index, height):
        return ref.at[pl.ds(pl.multiple_of(index * height, 8), height), :]

    def cell(ref, index, half):
        return slot(ref, index * HALVES + half, slim)

    def pair_cell(ref, index, r):
        return slot(ref, index * rounds + r, pair_slim)

    def load(k):
        span = pl.ds(k * piece, piece)
        return pltpu.make_async_copy(
            weight_hbm.at[span, :], weights.at[span, :], weight_sems.at[k]
        )

    barrier = pltpu.get_barrier_semaphore()

    @pl.loop(1, n)
    def _(o):
        pl.semaphore_signal(
            barrier, inc=1, device_id={"seq": lax.rem(me + o, n)},
            device_id_type=pl.DeviceIdType.MESH,
        )

    load_taps = pltpu.make_async_copy(taps_hbm, taps_ref, load_sems.at[0])
    load_x = pltpu.make_async_copy(x_hbm, x_ref, load_sems.at[1])
    load_grad = pltpu.make_async_copy(grad_hbm, grad_ref, load_sems.at[2])
    load_taps.start()
    load_x.start()
    load_grad.start()
    for k in range(PIECES):
        load(k).start()

    def taps_place(p, r):
        return (p * HALVES + r // per_half) * slim + r % per_half * cpr

    def pair_place(p, r, which):
        return (p * rounds + r) * pair_slim + which * cpr

    def spread(ref, values, place):
        for r in range(rounds):
            for p in range(n):
                at, first = place(p, r), r * few + p * cpr
                ref[at : at + cpr, :] = values[first : first + cpr, :]

    def gather(ref, place):
        return jnp.concatenate([ref[place(p) : place(p) + cpr, :] for p in range(n)], axis=0)

    anti = (
        lax.broadcasted_iota(jnp.int32, (rows, rows), 0)
        + lax.broadcasted_iota(jnp.int32, (rows, rows), 1)
        == rows - 1
    ).astype(f32)

    def reverse(values):
        return jnp.dot(
            values, anti, preferred_element_type=f32, precision=lax.Precision.HIGHEST
        )

    def taps_copy(h):
        def plan(peer, sender):
            return (remote(cell(send_taps, peer, h), cell(got_taps, sender, h),
                           sent_sems.at[TAPS, h], come_sems.at[TAPS, h], peer),)
        return plan

    def forth(r):
        def plan(peer, sender):
            return (remote(pair_cell(send_pair, peer, r), pair_cell(got_pair, sender, r),
                           sent_sems.at[FORTH, r], come_sems.at[FORTH, r], peer),)
        return plan

    def home(r):
        def plan(peer, sender):
            return (remote(pair_cell(made_pair, peer, r), pair_cell(home_pair, sender, r),
                           sent_sems.at[HOME, r], come_sems.at[HOME, r], peer),)
        return plan

    def home_last(h):
        def plan(peer, sender):
            return (remote(cell(made_taps, peer, h), cell(home_taps, sender, h),
                           sent_sems.at[LAST, h], come_sems.at[LAST, h], peer),)
        return plan

    def region(ref, height, send_sem, recv_sem):
        return remote(ref.at[pl.ds(0, height), :], ref.at[pl.ds(0, height), :],
                      send_sem, recv_sem, base + sibling)

    def exchange_start(plan):
        @pl.loop(1, n)
        def _(k):
            o = n - k
            peer = lax.rem(team + o // TEAM, teams) * TEAM + lax.rem(mine + o, TEAM)
            for copy in plan(peer, me):
                copy.start()

    def exchanged(kind, k):
        ref, height = (got_pair, pair_slim) if kind in (FORTH, HOME) else (got_taps, slim)
        return region(ref, (n - 1) * height, sent_sems.at[kind, k], come_sems.at[kind, k])

    def exchange_wait(kind, k):
        exchanged(kind, k).wait_recv()

    def exchange_sent(kind):
        for k in range(rounds if kind in (FORTH, HOME) else HALVES):
            exchanged(kind, k).wait_send()

    def cols(peer, index, sender, late):
        return remote(slot(send_cols, peer * teams + index, rows),
                      slot(got_cols, sender * teams + index, rows),
                      sent_sems.at[COLUMNS, 0], recv_cols_sems.at[late], base + peer)

    side = chip + 1 - 2 * lax.rem(chip, 2)
    pair = lax.rem(chip + 2, CHIPS)
    corner = lax.rem(side + 2, CHIPS)
    peers = (
        sibling,
        side * 2 + core, side * 2 + 1 - core,
        pair * 2 + core, pair * 2 + 1 - core,
        corner * 2 + core, corner * 2 + 1 - core,
    )

    def cols_start(late, chosen):
        @pl.loop(0 if late else 1, 1 if late else teams)
        def _(t):
            for k in chosen:
                cols(peers[k], lax.rem(team + t, teams), mine, late).start()

    def cols_wait(late):
        blocks = (TEAM - 1) * (1 if late else teams - 1)
        region(got_cols, blocks * rows, sent_sems.at[COLUMNS, 0], recv_cols_sems.at[late]).wait_recv()

    load_taps.wait()
    spread(send_taps, taps_ref[...].T, taps_place)
    load_x.wait()
    pl.semaphore_wait(barrier, n - 1)
    exchange_start(taps_copy(0))
    for g in range(TEAM):
        for t in range(teams):
            first = (t * TEAM + g) * block
            at = (g * teams + t) * rows
            send_cols[at : at + rows, :] = x_ref[:, first : first + block].astype(f32)
    cols_start(0, SOON)
    total = jnp.zeros((rows, KINDS * channels), f32)
    for k in range(PIECES):
        load(k).wait()
        total = total + jnp.dot(
            x_ref[:, k * piece : (k + 1) * piece], weights[k * piece : (k + 1) * piece, :],
            preferred_element_type=f32,
        )
    total = total.astype(bf16).astype(f32)
    load_grad.wait()
    spread(
        send_pair, (total[:, channels : 2 * channels] * total[:, 2 * channels :]).T,
        lambda p, r: pair_place(p, r, 0),
    )
    spread(
        send_pair, reverse((grad_ref[...].astype(f32) * total[:, :channels]).T),
        lambda p, r: pair_place(p, r, 1),
    )
    for r in range(rounds):
        if r > 0 and r % per_half == 0:
            exchange_start(taps_copy(r // per_half))
        exchange_start(forth(r))
    key_rows[...] = total[:, channels : 2 * channels]
    value_rows[...] = total[:, 2 * channels :]

    slot(got_cols, mine, teams * rows)[...] = slot(send_cols, mine, teams * rows)[...]
    slot(got_taps, me, HALVES * slim)[...] = slot(send_taps, me, HALVES * slim)[...]
    slot(got_pair, me, rounds * pair_slim)[...] = slot(send_pair, me, rounds * pair_slim)[...]
    pad_gated[pl.ds(0, n), :] = jnp.zeros((n, rows), f32)
    pad_back[pl.ds(n, n), :] = jnp.zeros((n, rows), f32)

    lane = lax.broadcasted_iota(jnp.int32, (rows, rows), 1)
    line = lax.broadcasted_iota(jnp.int32, (rows, rows), 0)
    keep = lane >= line
    group = min(GROUP, n)

    def turned(source, at, step, index):
        row = source[pl.ds(index * step + at, 1), :]
        return pltpu.roll(
            jnp.broadcast_to(row, (rows, rows)), 0, 1, stride=1, stride_axis=0
        )

    def channel(r, c):
        step = rounds * pair_slim
        at = r * pair_slim + c
        at_taps = r // per_half * slim + r % per_half * cpr + c
        here, there = pl.ds(at, n, stride=step), pl.ds(at + cpr, n, stride=step)
        pad_gated[pl.ds(n, n), :] = got_pair[here, :]
        pad_back[pl.ds(0, n), :] = got_pair[there, :]

        def some_lags(q, total):
            matrices = []
            for source, first, jump in ((got_taps, at_taps, HALVES * slim), (got_pair, at, step)):
                if isinstance(q, int):
                    before = jnp.zeros((rows, rows), f32)
                else:
                    before = turned(source, first, jump, jnp.maximum(q * group - 1, 0))
                    before = jnp.where(q == 0, 0.0, before)
                parts = []
                for e in range(group):
                    now = turned(source, first, jump, q * group + e)
                    parts.append(jnp.where(keep, now, before).astype(bf16))
                    before = now
                matrices.append(jnp.concatenate(parts, axis=0))
            table = jnp.concatenate(matrices, axis=1)
            lines = jnp.concatenate(
                [
                    jnp.concatenate(
                        [ref[pl.ds(first + sign * (q * group + e), n), :] for e in range(group)],
                        axis=1,
                    ).astype(bf16)
                    for ref, first, sign in ((pad_gated, n, -1), (pad_back, 0, 1))
                ],
                axis=0,
            )
            return total + jnp.dot(lines, table, preferred_element_type=f32)

        sums = jnp.zeros((2 * n, 2 * rows), f32)
        if n == group:
            sums = some_lags(0, sums)
        else:
            sums = lax.fori_loop(0, n // group, some_lags, sums)
        made_pair[here, :] = sums[:n, :rows]
        made_pair[there, :] = sums[n:, :rows]
        made_taps[pl.ds(at_taps, n, stride=HALVES * slim), :] = sums[n:, rows:]

    def convolve(r):
        if r % per_half == 0:
            exchange_wait(TAPS, r // per_half)
        exchange_wait(FORTH, r)

        @pl.loop(0, cpr)
        def _(c):
            channel(r, c)

        exchange_start(home(r))
        if (r + 1) % per_half == 0:
            h = r // per_half
            exchange_start(home_last(h))
            cell(home_taps, me, h)[...] = cell(made_taps, me, h)[...]
        pair_cell(home_pair, me, r)[...] = pair_cell(made_pair, me, r)[...]

    def turn_columns(index):
        for s in range(TEAM):
            left[pl.ds(pl.multiple_of(index * block, 16), block), s * rows : (s + 1) * rows] = (
                slot(got_cols, s * teams + index, rows)[...].T.astype(bf16)
            )

    def held(part, member):
        return slot(proj_all, part * TEAM + member, rows)

    chunks = rounds * KINDS // PARTS

    def spans_of(part):
        spans = []
        for j in range(chunks):
            r, kind = divmod(part * chunks + j, KINDS)
            spans.append((slice(j * few, (j + 1) * few), kind * channels + r * few))
        return [(inside, slice(first, first + few)) for inside, first in spans]

    def make_values(r):
        exchange_wait(HOME, r)
        conv = reverse(gather(home_pair, lambda p: pair_place(p, r, 1))).T * scaling
        mixed = gather(home_pair, lambda p: pair_place(p, r, 0)).T * scaling
        span = slice(r * few, (r + 1) * few)
        for kind, values in enumerate((
            grad_ref[:, span].astype(f32) * mixed,
            conv * value_rows[:, span],
            conv * key_rows[:, span],
        )):
            part, j = divmod(r * KINDS + kind, chunks)
            held(part, mine)[:, j * few : (j + 1) * few] = values.astype(bf16).astype(f32)

    def spread_copy(part, k):
        member, target = (
            (mine, pair * 2 + core),
            (mine, side * 2 + core),
            (mine, sibling),
            (pair * 2 + core, side * 2 + core),
            (pair * 2 + core, sibling),
            (side * 2 + core, sibling),
            (corner * 2 + core, sibling),
        )[k]
        return remote(held(part, member), held(part, member), sent_sems.at[SPREAD, 0],
                      recv_sems.at[part, (0, 1, 3, 2, 3, 3, 3)[k]], base + target)

    def arrived(part, k):
        blocks = TEAM // 2 if k == 3 else 1
        region(proj_all, blocks * rows, sent_sems.at[SPREAD, 0], recv_sems.at[part, k]).wait_recv()

    def spread_first(part):
        for k in range(3):
            spread_copy(part, k).start()

    def spread_second(part):
        arrived(part, 0)
        spread_copy(part, 3).start()
        spread_copy(part, 4).start()
        arrived(part, 1)
        spread_copy(part, 5).start()

    def spread_third(part):
        arrived(part, 2)
        spread_copy(part, 6).start()
        arrived(part, 3)

    def sums_copy(part, to_team, from_team, peer):
        return remote(slot(made, part * teams + to_team, block),
                      slot(got, part * teams + from_team, block),
                      sent_sems.at[SUMS, 0], recv_sum_sems.at[part],
                      peer * TEAM + mine)

    def product(part, index):
        lines = left[pl.ds(pl.multiple_of(index * block, 16), block), :]
        right = proj_all[part * TEAM * rows : (part + 1) * TEAM * rows, :].astype(bf16)
        return jnp.dot(lines, right, preferred_element_type=f32)

    def send_products(part):
        @pl.loop(1, teams)
        def _(o):
            target = lax.rem(team + o, teams)
            slot(made, part * teams + target, block)[...] = product(part, target)
            sums_copy(part, target, team, target).start()

    def first_columns(chosen):
        cols_start(0, chosen)

    def late_columns(chosen):
        cols_start(1, chosen)

    def turn_first(_):
        cols_wait(0)

        @pl.loop(1, teams)
        def _(t):
            turn_columns(lax.rem(team + t, teams))

    if rounds == 4:
        steps = (
            (first_columns, (4, 2)), (convolve, 0), (first_columns, (5,)), (convolve, 1),
            (make_values, 0), (spread_first, 0), (first_columns, (6, 0)), (convolve, 2),
            (make_values, 1), (spread_second, 0), (spread_first, 1), (spread_first, 2),
            (convolve, 3), (make_values, 2), (spread_first, 3), (spread_second, 1),
            (turn_first, 0), (spread_third, 0), (send_products, 0), (late_columns, (3,)),
            (spread_second, 2), (make_values, 3), (spread_first, 4), (spread_third, 1),
            (send_products, 1), (late_columns, (1, 4)), (spread_first, 5), (spread_second, 3),
            (spread_third, 2), (send_products, 2), (late_columns, (2, 5)), (spread_second, 4),
            (spread_third, 3), (send_products, 3), (late_columns, (0, 6)), (spread_second, 5),
            (spread_third, 4), (send_products, 4), (spread_third, 5), (send_products, 5),
        )
    else:
        steps = (
            [(first_columns, REST)]
            + [(convolve, r) for r in range(rounds)]
            + [(make_values, r) for r in range(rounds)]
            + [(spread_first, p) for p in range(PARTS)]
            + [(turn_first, 0), (late_columns, SOON + REST)]
            + [(act, p) for p in range(PARTS) for act in (spread_second, spread_third, send_products)]
        )
    for act, given in steps:
        act(given)

    tile = min(512, depth)
    lines = jnp.concatenate(
        [
            held((r * KINDS + kind) // chunks, mine)[
                :, (r * KINDS + kind) % chunks * few : ((r * KINDS + kind) % chunks + 1) * few
            ].astype(bf16)
            for kind in range(KINDS)
            for r in range(rounds)
        ],
        axis=1,
    )

    @pl.loop(0, depth // tile)
    def _(t):
        start = pl.multiple_of(t * tile, tile)
        grad_inputs_ref[:, pl.ds(start, tile)] = lax.dot_general(
            lines, weights[pl.ds(start, tile), :], (((1,), (1,)), ((), ())),
            preferred_element_type=f32,
        ).astype(bf16)

    for h in range(HALVES):
        exchange_wait(LAST, h)
    for r in range(rounds):
        grad_taps_ref[:, r * few : (r + 1) * few] = (
            reverse(gather(home_taps, lambda p: taps_place(p, r))).T * scaling
        )

    cols_wait(1)
    turn_columns(team)
    for part in range(PARTS):
        made_here = product(part, team)
        for inside, span in spans_of(part):
            out_ref[:, span] = made_here[:, inside]

    for kind in (TAPS, FORTH, HOME, LAST):
        exchange_sent(kind)
    region(got_cols, (TEAM - 1) * teams * rows, sent_sems.at[COLUMNS, 0],
           recv_cols_sems.at[0]).wait_send()
    region(proj_all, PARTS * 7 * rows, sent_sems.at[SPREAD, 0], recv_sems.at[0, 0]).wait_send()

    for part in range(PARTS):
        region(got, (teams - 1) * block, sent_sems.at[SUMS, 0], recv_sum_sems.at[part]).wait_recv()

        for inside, span in spans_of(part):
            kept = out_ref[:, span]
            if teams == 2:
                kept = kept + slot(got, part * teams + 1 - team, block)[:, inside]
            else:
                def add_one(o, kept):
                    other = lax.rem(team + o, teams)
                    return kept + slot(got, part * teams + other, block)[:, inside]

                kept = lax.fori_loop(1, teams, add_one, kept)
            out_ref[:, span] = kept * scaling

    region(got, PARTS * (teams - 1) * block, sent_sems.at[SUMS, 0], recv_sum_sems.at[0]).wait_send()


def write_kernel(*refs):
    sems = refs[-1]
    copies = [pltpu.make_async_copy(refs[k], refs[3 + k], sems.at[k]) for k in range(3)]
    for copy in copies:
        copy.start()
    for copy in copies:
        copy.wait()


def per_device(inputs, in_weight, filter_taps, grad_out):
    rows, depth = inputs.shape
    channels = filter_taps.shape[1]
    n = lax.axis_size("seq")
    teams = n // TEAM
    scaling = 1.0 / math.sqrt(rows * n)
    width = channels // HALVES
    rounds = rounds_of(channels, n)
    cpr = channels // rounds // n
    slim = round_up(cpr * (rounds // HALVES), 8)
    pair_slim = round_up(2 * cpr, 8)
    half, whole = n * HALVES * slim, n * rounds * pair_slim
    block = depth // n
    f32, bf16 = jnp.float32, jnp.bfloat16
    vmem = pl.BlockSpec(memory_space=pltpu.VMEM)
    anywhere = pl.BlockSpec(memory_space=pl.ANY)
    dma = pltpu.SemaphoreType.DMA
    results = pl.pallas_call(
        functools.partial(fused_kernel, n, scaling),
        out_shape=(
            pltpu.VMEM((rows, depth), bf16),
            pltpu.VMEM((block, KINDS * channels), f32),
            pltpu.VMEM((rows, channels), f32),
        ),
        in_specs=[anywhere] * 4,
        out_specs=(vmem,) * 3,
        scratch_shapes=[
            pltpu.VMEM(inputs.shape, inputs.dtype),
            pltpu.VMEM(in_weight.shape, in_weight.dtype),
            pltpu.VMEM(filter_taps.shape, filter_taps.dtype),
            pltpu.VMEM(grad_out.shape, grad_out.dtype),
        ]
        + [
            pltpu.VMEM((height, rows), f32)
            for height in (half, whole, half, whole, whole, half, whole, half)
        ]
        + [
            pltpu.VMEM((2 * n, rows), f32),
            pltpu.VMEM((2 * n, rows), f32),
            pltpu.VMEM((n * rows, block), f32),
            pltpu.VMEM((n * rows, block), f32),
            pltpu.VMEM((teams * block, TEAM * rows), bf16),
            pltpu.VMEM((rows, channels), f32),
            pltpu.VMEM((rows, channels), f32),
            pltpu.VMEM((PARTS * TEAM * rows, width), f32),
            pltpu.VMEM((PARTS * teams * block, width), f32),
            pltpu.VMEM((PARTS * teams * block, width), f32),
            dma((3,)), dma((PIECES,)), dma((7, rounds)), dma((4, rounds)), dma((2,)),
            dma((PARTS, 4)), dma((PARTS,)),
        ],
        compiler_params=pltpu.CompilerParams(
            collective_id=0, has_side_effects=True, vmem_limit_bytes=117 << 19
        ),
    )(inputs, in_weight, filter_taps, grad_out)
    return pl.pallas_call(
        write_kernel,
        out_shape=tuple(jax.ShapeDtypeStruct(r.shape, r.dtype) for r in results),
        in_specs=[anywhere] * 3,
        out_specs=(anywhere,) * 3,
        scratch_shapes=[dma((3,))],
        compiler_params=pltpu.CompilerParams(vmem_limit_bytes=2 << 20),
    )(*results)


def solution(mesh):
    in_specs = (P(("grp", "seq"), None), P(), P("seq", None), P(("grp", "seq"), None))
    out_specs = (P(("grp", "seq"), None), P(("grp", "seq"), None), P(("grp", "seq"), None))
    return jax.shard_map(
        per_device, mesh=mesh, in_specs=in_specs, out_specs=out_specs, check_vma=False
    )
```

```python
import functools
import math

import jax
import jax.numpy as jnp
from jax import lax
from jax.experimental import pallas as pl
from jax.experimental.pallas import tpu as pltpu
from jax.sharding import PartitionSpec as P

GROUP = 16
TEAM = 8
CHIPS = 4
HALVES = 2
KINDS = 3
PARTS = HALVES * KINDS
PIECES = 2
SOON, REST = (3, 1), (0, 2, 4, 5, 6)
TAPS, FORTH, HOME, LAST, COLUMNS, SPREAD, SUMS = range(7)


def round_up(value, step):
    return (value + step - 1) // step * step


def rounds_of(channels, n):
    return 4 if channels // n % 4 == 0 else HALVES


def remote(src, dst, send_sem, recv_sem, peer):
    return pltpu.make_async_remote_copy(
        src_ref=src,
        dst_ref=dst,
        send_sem=send_sem,
        recv_sem=recv_sem,
        device_id={"seq": peer},
        device_id_type=pl.DeviceIdType.MESH,
    )


def fused_kernel(
    n, scaling, x_hbm, weight_hbm, taps_hbm, grad_hbm,
    grad_inputs_ref, out_ref, grad_taps_ref,
    x_ref, weights, taps_ref, grad_ref,
    send_taps, send_pair, got_taps, got_pair, made_pair, made_taps, home_pair, home_taps,
    pad_gated, pad_back, send_cols, got_cols, left, key_rows, value_rows,
    proj_all, made, got,
    load_sems, weight_sems, sent_sems, come_sems, recv_cols_sems, recv_sems, recv_sum_sems,
):
    f32, bf16 = jnp.float32, jnp.bfloat16
    me = lax.axis_index("seq")
    rows, depth = x_ref.shape
    channels = taps_ref.shape[1]
    width = channels // HALVES
    rounds = rounds_of(channels, n)
    few = channels // rounds
    cpr = few // n
    per_half = rounds // HALVES
    slim = round_up(cpr * per_half, 8)
    pair_slim = round_up(2 * cpr, 8)
    teams = n // TEAM
    team, mine = me // TEAM, lax.rem(me, TEAM)
    base, chip, core = team * TEAM, mine // 2, lax.rem(mine, 2)
    sibling = chip * 2 + 1 - core
    block = depth // n
    piece = depth // PIECES

    def slot(ref, index, height):
        return ref.at[pl.ds(pl.multiple_of(index * height, 8), height), :]

    def cell(ref, index, half):
        return slot(ref, index * HALVES + half, slim)

    def pair_cell(ref, index, r):
        return slot(ref, index * rounds + r, pair_slim)

    def load(k):
        span = pl.ds(k * piece, piece)
        return pltpu.make_async_copy(
            weight_hbm.at[span, :], weights.at[span, :], weight_sems.at[k]
        )

    barrier = pltpu.get_barrier_semaphore()

    @pl.loop(1, n)
    def _(o):
        pl.semaphore_signal(
            barrier, inc=1, device_id={"seq": lax.rem(me + o, n)},
            device_id_type=pl.DeviceIdType.MESH,
        )

    load_taps = pltpu.make_async_copy(taps_hbm, taps_ref, load_sems.at[0])
    load_x = pltpu.make_async_copy(x_hbm, x_ref, load_sems.at[1])
    load_grad = pltpu.make_async_copy(grad_hbm, grad_ref, load_sems.at[2])
    load_taps.start()
    load_x.start()
    load_grad.start()
    for k in range(PIECES):
        load(k).start()

    def taps_place(p, r):
        return (p * HALVES + r // per_half) * slim + r % per_half * cpr

    def pair_place(p, r, which):
        return (p * rounds + r) * pair_slim + which * cpr

    def spread(ref, values, place):
        for r in range(rounds):
            for p in range(n):
                at, first = place(p, r), r * few + p * cpr
                ref[at : at + cpr, :] = values[first : first + cpr, :]

    def gather(ref, place):
        return jnp.concatenate([ref[place(p) : place(p) + cpr, :] for p in range(n)], axis=0)

    anti = (
        lax.broadcasted_iota(jnp.int32, (rows, rows), 0)
        + lax.broadcasted_iota(jnp.int32, (rows, rows), 1)
        == rows - 1
    ).astype(f32)

    def reverse(values):
        return jnp.dot(
            values, anti, preferred_element_type=f32, precision=lax.Precision.HIGHEST
        )

    def taps_copy(h):
        def plan(peer, sender):
            return (remote(cell(send_taps, peer, h), cell(got_taps, sender, h),
                           sent_sems.at[TAPS, h], come_sems.at[TAPS, h], peer),)
        return plan

    def forth(r):
        def plan(peer, sender):
            return (remote(pair_cell(send_pair, peer, r), pair_cell(got_pair, sender, r),
                           sent_sems.at[FORTH, r], come_sems.at[FORTH, r], peer),)
        return plan

    def home(r):
        def plan(peer, sender):
            return (remote(pair_cell(made_pair, peer, r), pair_cell(home_pair, sender, r),
                           sent_sems.at[HOME, r], come_sems.at[HOME, r], peer),)
        return plan

    def home_last(h):
        def plan(peer, sender):
            return (remote(cell(made_taps, peer, h), cell(home_taps, sender, h),
                           sent_sems.at[LAST, h], come_sems.at[LAST, h], peer),)
        return plan

    def region(ref, height, send_sem, recv_sem):
        return remote(ref.at[pl.ds(0, height), :], ref.at[pl.ds(0, height), :],
                      send_sem, recv_sem, base + sibling)

    def exchange_start(plan):
        @pl.loop(1, n)
        def _(k):
            o = n - k
            peer = lax.rem(team + o // TEAM, teams) * TEAM + lax.rem(mine + o, TEAM)
            for copy in plan(peer, me):
                copy.start()

    def exchanged(kind, k):
        ref, height = (got_pair, pair_slim) if kind in (FORTH, HOME) else (got_taps, slim)
        return region(ref, (n - 1) * height, sent_sems.at[kind, k], come_sems.at[kind, k])

    def exchange_wait(kind, k):
        exchanged(kind, k).wait_recv()

    def exchange_sent(kind):
        for k in range(rounds if kind in (FORTH, HOME) else HALVES):
            exchanged(kind, k).wait_send()

    def cols(peer, index, sender, late):
        return remote(slot(send_cols, peer * teams + index, rows),
                      slot(got_cols, sender * teams + index, rows),
                      sent_sems.at[COLUMNS, 0], recv_cols_sems.at[late], base + peer)

    side = chip + 1 - 2 * lax.rem(chip, 2)
    pair = lax.rem(chip + 2, CHIPS)
    corner = lax.rem(side + 2, CHIPS)
    peers = (
        sibling,
        side * 2 + core, side * 2 + 1 - core,
        pair * 2 + core, pair * 2 + 1 - core,
        corner * 2 + core, corner * 2 + 1 - core,
    )

    def cols_start(late, chosen):
        @pl.loop(0 if late else 1, 1 if late else teams)
        def _(t):
            for k in chosen:
                cols(peers[k], lax.rem(team + t, teams), mine, late).start()

    def cols_wait(late):
        blocks = (TEAM - 1) * (1 if late else teams - 1)
        region(got_cols, blocks * rows, sent_sems.at[COLUMNS, 0], recv_cols_sems.at[late]).wait_recv()

    load_taps.wait()
    spread(send_taps, taps_ref[...].T, taps_place)
    load_x.wait()
    pl.semaphore_wait(barrier, n - 1)
    exchange_start(taps_copy(0))
    for g in range(TEAM):
        for t in range(teams):
            first = (t * TEAM + g) * block
            at = (g * teams + t) * rows
            send_cols[at : at + rows, :] = x_ref[:, first : first + block].astype(f32)
    cols_start(0, SOON)
    total = jnp.zeros((rows, KINDS * channels), f32)
    for k in range(PIECES):
        load(k).wait()
        total = total + jnp.dot(
            x_ref[:, k * piece : (k + 1) * piece], weights[k * piece : (k + 1) * piece, :],
            preferred_element_type=f32,
        )
    total = total.astype(bf16).astype(f32)
    load_grad.wait()
    spread(
        send_pair, (total[:, channels : 2 * channels] * total[:, 2 * channels :]).T,
        lambda p, r: pair_place(p, r, 0),
    )
    spread(
        send_pair, reverse((grad_ref[...].astype(f32) * total[:, :channels]).T),
        lambda p, r: pair_place(p, r, 1),
    )
    for r in range(rounds):
        if r > 0 and r % per_half == 0:
            exchange_start(taps_copy(r // per_half))
        exchange_start(forth(r))
    key_rows[...] = total[:, channels : 2 * channels]
    value_rows[...] = total[:, 2 * channels :]

    slot(got_cols, mine, teams * rows)[...] = slot(send_cols, mine, teams * rows)[...]
    slot(got_taps, me, HALVES * slim)[...] = slot(send_taps, me, HALVES * slim)[...]
    slot(got_pair, me, rounds * pair_slim)[...] = slot(send_pair, me, rounds * pair_slim)[...]
    pad_gated[pl.ds(0, n), :] = jnp.zeros((n, rows), f32)
    pad_back[pl.ds(n, n), :] = jnp.zeros((n, rows), f32)

    lane = lax.broadcasted_iota(jnp.int32, (rows, rows), 1)
    line = lax.broadcasted_iota(jnp.int32, (rows, rows), 0)
    keep = lane >= line
    group = min(GROUP, n)

    def turned(source, at, step, index):
        row = source[pl.ds(index * step + at, 1), :]
        return pltpu.roll(
            jnp.broadcast_to(row, (rows, rows)), 0, 1, stride=1, stride_axis=0
        )

    def channel(r, c):
        step = rounds * pair_slim
        at = r * pair_slim + c
        at_taps = r // per_half * slim + r % per_half * cpr + c
        here, there = pl.ds(at, n, stride=step), pl.ds(at + cpr, n, stride=step)
        pad_gated[pl.ds(n, n), :] = got_pair[here, :]
        pad_back[pl.ds(0, n), :] = got_pair[there, :]

        def some_lags(q, total):
            matrices = []
            for source, first, jump in ((got_taps, at_taps, HALVES * slim), (got_pair, at, step)):
                if isinstance(q, int):
                    before = jnp.zeros((rows, rows), f32)
                else:
                    before = turned(source, first, jump, jnp.maximum(q * group - 1, 0))
                    before = jnp.where(q == 0, 0.0, before)
                parts = []
                for e in range(group):
                    now = turned(source, first, jump, q * group + e)
                    parts.append(jnp.where(keep, now, before).astype(bf16))
                    before = now
                matrices.append(jnp.concatenate(parts, axis=0))
            table = jnp.concatenate(matrices, axis=1)
            lines = jnp.concatenate(
                [
                    jnp.concatenate(
                        [ref[pl.ds(first + sign * (q * group + e), n), :] for e in range(group)],
                        axis=1,
                    ).astype(bf16)
                    for ref, first, sign in ((pad_gated, n, -1), (pad_back, 0, 1))
                ],
                axis=0,
            )
            return total + jnp.dot(lines, table, preferred_element_type=f32)

        sums = jnp.zeros((2 * n, 2 * rows), f32)
        if n == group:
            sums = some_lags(0, sums)
        else:
            sums = lax.fori_loop(0, n // group, some_lags, sums)
        made_pair[here, :] = sums[:n, :rows]
        made_pair[there, :] = sums[n:, :rows]
        made_taps[pl.ds(at_taps, n, stride=HALVES * slim), :] = sums[n:, rows:]

    def convolve(r):
        if r % per_half == 0:
            exchange_wait(TAPS, r // per_half)
        exchange_wait(FORTH, r)

        @pl.loop(0, cpr)
        def _(c):
            channel(r, c)

        exchange_start(home(r))
        if (r + 1) % per_half == 0:
            h = r // per_half
            exchange_start(home_last(h))
            cell(home_taps, me, h)[...] = cell(made_taps, me, h)[...]
        pair_cell(home_pair, me, r)[...] = pair_cell(made_pair, me, r)[...]

    def turn_columns(index):
        for s in range(TEAM):
            left[pl.ds(pl.multiple_of(index * block, 16), block), s * rows : (s + 1) * rows] = (
                slot(got_cols, s * teams + index, rows)[...].T.astype(bf16)
            )

    def held(part, member):
        return slot(proj_all, part * TEAM + member, rows)

    chunks = rounds * KINDS // PARTS

    def spans_of(part):
        spans = []
        for j in range(chunks):
            r, kind = divmod(part * chunks + j, KINDS)
            spans.append((slice(j * few, (j + 1) * few), kind * channels + r * few))
        return [(inside, slice(first, first + few)) for inside, first in spans]

    def make_values(r):
        exchange_wait(HOME, r)
        conv = reverse(gather(home_pair, lambda p: pair_place(p, r, 1))).T * scaling
        mixed = gather(home_pair, lambda p: pair_place(p, r, 0)).T * scaling
        span = slice(r * few, (r + 1) * few)
        for kind, values in enumerate((
            grad_ref[:, span].astype(f32) * mixed,
            conv * value_rows[:, span],
            conv * key_rows[:, span],
        )):
            part, j = divmod(r * KINDS + kind, chunks)
            held(part, mine)[:, j * few : (j + 1) * few] = values.astype(bf16).astype(f32)

    def spread_copy(part, k):
        member, target = (
            (mine, pair * 2 + core),
            (mine, side * 2 + core),
            (mine, sibling),
            (pair * 2 + core, side * 2 + core),
            (pair * 2 + core, sibling),
            (side * 2 + core, sibling),
            (corner * 2 + core, sibling),
        )[k]
        return remote(held(part, member), held(part, member), sent_sems.at[SPREAD, 0],
                      recv_sems.at[part, (0, 1, 3, 2, 3, 3, 3)[k]], base + target)

    def arrived(part, k):
        blocks = TEAM // 2 if k == 3 else 1
        region(proj_all, blocks * rows, sent_sems.at[SPREAD, 0], recv_sems.at[part, k]).wait_recv()

    def spread_first(part):
        for k in range(3):
            spread_copy(part, k).start()

    def spread_second(part):
        arrived(part, 0)
        spread_copy(part, 3).start()
        spread_copy(part, 4).start()
        arrived(part, 1)
        spread_copy(part, 5).start()

    def spread_third(part):
        arrived(part, 2)
        spread_copy(part, 6).start()
        arrived(part, 3)

    def sums_copy(part, to_team, from_team, peer):
        return remote(slot(made, part * teams + to_team, block),
                      slot(got, part * teams + from_team, block),
                      sent_sems.at[SUMS, 0], recv_sum_sems.at[part],
                      peer * TEAM + mine)

    def product(part, index):
        lines = left[pl.ds(pl.multiple_of(index * block, 16), block), :]
        right = proj_all[part * TEAM * rows : (part + 1) * TEAM * rows, :].astype(bf16)
        return jnp.dot(lines, right, preferred_element_type=f32)

    def send_products(part):
        @pl.loop(1, teams)
        def _(o):
            target = lax.rem(team + o, teams)
            slot(made, part * teams + target, block)[...] = product(part, target)
            sums_copy(part, target, team, target).start()

    def first_columns(chosen):
        cols_start(0, chosen)

    def late_columns(chosen):
        cols_start(1, chosen)

    def turn_first(_):
        cols_wait(0)

        @pl.loop(1, teams)
        def _(t):
            turn_columns(lax.rem(team + t, teams))

    if rounds == 4:
        steps = (
            (first_columns, (4, 2)), (convolve, 0), (first_columns, (5,)), (convolve, 1),
            (make_values, 0), (spread_first, 0), (first_columns, (6, 0)), (convolve, 2),
            (make_values, 1), (spread_second, 0), (spread_first, 1), (spread_first, 2),
            (convolve, 3), (make_values, 2), (spread_first, 3), (spread_second, 1),
            (turn_first, 0), (spread_third, 0), (send_products, 0), (late_columns, (3,)),
            (spread_second, 2), (make_values, 3), (spread_first, 4), (spread_third, 1),
            (send_products, 1), (late_columns, (1, 4)), (spread_first, 5), (spread_second, 3),
            (spread_third, 2), (send_products, 2), (late_columns, (2, 5)), (spread_second, 4),
            (spread_third, 3), (send_products, 3), (late_columns, (0, 6)), (spread_second, 5),
            (spread_third, 4), (send_products, 4), (spread_third, 5), (send_products, 5),
        )
    else:
        steps = (
            [(first_columns, REST)]
            + [(convolve, r) for r in range(rounds)]
            + [(make_values, r) for r in range(rounds)]
            + [(spread_first, p) for p in range(PARTS)]
            + [(turn_first, 0), (late_columns, SOON + REST)]
            + [(act, p) for p in range(PARTS) for act in (spread_second, spread_third, send_products)]
        )
    for act, given in steps:
        act(given)

    tile = min(512, depth)
    lines = jnp.concatenate(
        [
            held((r * KINDS + kind) // chunks, mine)[
                :, (r * KINDS + kind) % chunks * few : ((r * KINDS + kind) % chunks + 1) * few
            ].astype(bf16)
            for kind in range(KINDS)
            for r in range(rounds)
        ],
        axis=1,
    )

    @pl.loop(0, depth // tile)
    def _(t):
        start = pl.multiple_of(t * tile, tile)
        grad_inputs_ref[:, pl.ds(start, tile)] = lax.dot_general(
            lines, weights[pl.ds(start, tile), :], (((1,), (1,)), ((), ())),
            preferred_element_type=f32,
        ).astype(bf16)

    for h in range(HALVES):
        exchange_wait(LAST, h)
    for r in range(rounds):
        grad_taps_ref[:, r * few : (r + 1) * few] = (
            reverse(gather(home_taps, lambda p: taps_place(p, r))).T * scaling
        )

    cols_wait(1)
    turn_columns(team)
    for part in range(PARTS):
        made_here = product(part, team)
        for inside, span in spans_of(part):
            out_ref[:, span] = made_here[:, inside]

    for kind in (TAPS, FORTH, HOME, LAST):
        exchange_sent(kind)
    region(got_cols, (TEAM - 1) * teams * rows, sent_sems.at[COLUMNS, 0],
           recv_cols_sems.at[0]).wait_send()
    region(proj_all, PARTS * 7 * rows, sent_sems.at[SPREAD, 0], recv_sems.at[0, 0]).wait_send()

    for part in range(PARTS):
        region(got, (teams - 1) * block, sent_sems.at[SUMS, 0], recv_sum_sems.at[part]).wait_recv()

        for inside, span in spans_of(part):
            kept = out_ref[:, span]
            if teams == 2:
                kept = kept + slot(got, part * teams + 1 - team, block)[:, inside]
            else:
                def add_one(o, kept):
                    other = lax.rem(team + o, teams)
                    return kept + slot(got, part * teams + other, block)[:, inside]

                kept = lax.fori_loop(1, teams, add_one, kept)
            out_ref[:, span] = kept * scaling

    region(got, PARTS * (teams - 1) * block, sent_sems.at[SUMS, 0], recv_sum_sems.at[0]).wait_send()


def write_kernel(*refs):
    sems = refs[-1]
    copies = [pltpu.make_async_copy(refs[k], refs[3 + k], sems.at[k]) for k in range(3)]
    for copy in copies:
        copy.start()
    for copy in copies:
        copy.wait()


def per_device(inputs, in_weight, filter_taps, grad_out):
    rows, depth = inputs.shape
    channels = filter_taps.shape[1]
    n = lax.axis_size("seq")
    teams = n // TEAM
    scaling = 1.0 / math.sqrt(rows * n)
    width = channels // HALVES
    rounds = rounds_of(channels, n)
    cpr = channels // rounds // n
    slim = round_up(cpr * (rounds // HALVES), 8)
    pair_slim = round_up(2 * cpr, 8)
    half, whole = n * HALVES * slim, n * rounds * pair_slim
    block = depth // n
    f32, bf16 = jnp.float32, jnp.bfloat16
    vmem = pl.BlockSpec(memory_space=pltpu.VMEM)
    anywhere = pl.BlockSpec(memory_space=pl.ANY)
    dma = pltpu.SemaphoreType.DMA
    results = pl.pallas_call(
        functools.partial(fused_kernel, n, scaling),
        out_shape=(
            pltpu.VMEM((rows, depth), bf16),
            pltpu.VMEM((block, KINDS * channels), f32),
            pltpu.VMEM((rows, channels), f32),
        ),
        in_specs=[anywhere] * 4,
        out_specs=(vmem,) * 3,
        scratch_shapes=[
            pltpu.VMEM(inputs.shape, inputs.dtype),
            pltpu.VMEM(in_weight.shape, in_weight.dtype),
            pltpu.VMEM(filter_taps.shape, filter_taps.dtype),
            pltpu.VMEM(grad_out.shape, grad_out.dtype),
        ]
        + [
            pltpu.VMEM((height, rows), f32)
            for height in (half, whole, half, whole, whole, half, whole, half)
        ]
        + [
            pltpu.VMEM((2 * n, rows), f32),
            pltpu.VMEM((2 * n, rows), f32),
            pltpu.VMEM((n * rows, block), f32),
            pltpu.VMEM((n * rows, block), f32),
            pltpu.VMEM((teams * block, TEAM * rows), bf16),
            pltpu.VMEM((rows, channels), f32),
            pltpu.VMEM((rows, channels), f32),
            pltpu.VMEM((PARTS * TEAM * rows, width), f32),
            pltpu.VMEM((PARTS * teams * block, width), f32),
            pltpu.VMEM((PARTS * teams * block, width), f32),
            dma((3,)), dma((PIECES,)), dma((7, rounds)), dma((4, rounds)), dma((2,)),
            dma((PARTS, 4)), dma((PARTS,)),
        ],
        compiler_params=pltpu.CompilerParams(
            collective_id=0, has_side_effects=True, vmem_limit_bytes=117 << 19
        ),
    )(inputs, in_weight, filter_taps, grad_out)
    return pl.pallas_call(
        write_kernel,
        out_shape=tuple(jax.ShapeDtypeStruct(r.shape, r.dtype) for r in results),
        in_specs=[anywhere] * 3,
        out_specs=(anywhere,) * 3,
        scratch_shapes=[dma((3,))],
        compiler_params=pltpu.CompilerParams(vmem_limit_bytes=2 << 20),
    )(*results)


def solution(mesh):
    in_specs = (P(("grp", "seq"), None), P(), P("seq", None), P(("grp", "seq"), None))
    out_specs = (P(("grp", "seq"), None), P(("grp", "seq"), None), P(("grp", "seq"), None))
    return jax.shard_map(
        per_device, mesh=mesh, in_specs=in_specs, out_specs=out_specs, check_vma=False
    )
```
